256 devices in a mesh: sec: 128 (over x, y, z), tile: 2 (over core).
Axes of the slice: x: 4, y: 4, z: 8, core: 2. Of those that a mesh axis runs over, the one named last changes fastest.
Arguments:
- sections: bfloat16 [128, 256, 4096], P('sec', None, 'tile'), may hold values from -120 to 120, as said below
- calibration_knots: int32 [17], replicated, may hold values from 200 to 8200, as said below
- target_offset: int32 [4, 64], P(None, 'tile'), may hold values from 0 to 63
- target_step: int32 [4, 64], P(None, 'tile'), may hold values from 32 to 63
Outputs:
- resampled: bfloat16 [128, 256, 4096], P(None, 'sec', 'tile')
The draws below stay inside these ranges and needn't reach their ends.
Inputs may be any that keep to these rules, and one draw needn't show every extreme that they name: sections are intensities correlated from section to section. calibration_knots fall strictly from the first knot, 8200, to the last, 200.
All inputs are finite; a program needn't handle non-finite values.
Results may differ from the reference program's by a relative error of at most 0.0044.
Values may be sent and summed in bfloat16 or wider, within the bound.
A program may use at most 256 MiB of HBM per device.

```python
import jax
import jax.numpy as jnp
from jax import lax

COLS = 4096
TILE = 64
AHEAD = 4
KNOTS = 17
ROWS = 256
NSEC = 128
NOUT = 128
TR = 4
TC = 64


def draw_sections(key, part):
    key_base, key_jitter, key_noise = jax.random.split(key, 3)
    tile_rows = ROWS // TILE
    tile_cols = COLS // TILE
    baseline = jax.random.uniform(key_base, (tile_rows, tile_cols), jnp.float32, 0.35, 0.95)
    jitter = jax.random.uniform(key_jitter, (NSEC, tile_rows, tile_cols), jnp.float32, 0.6, 1.0)
    factors = baseline[None] * jitter
    tile_scale = jnp.ones((tile_rows, tile_cols), jnp.float32)
    tile_shift = jnp.zeros((tile_rows, tile_cols), jnp.float32)
    scale_pixels = jnp.repeat(jnp.repeat(tile_scale, TILE, 0), TILE, 1)
    shift_pixels = jnp.repeat(jnp.repeat(tile_shift, TILE, 0), TILE, 1)
    layer_keys = jax.random.split(key_noise, NSEC)

    def advance(previous, layer):
        factor_tile, layer_key = layer
        spread = jnp.repeat(jnp.repeat(factor_tile, TILE, 0), TILE, 1)
        noise = jnp.clip(jax.random.normal(layer_key, (ROWS, COLS), jnp.float32), -6.0, 6.0)
        current = spread * previous + jnp.sqrt(1.0 - spread * spread) * noise
        drawn = current * scale_pixels + shift_pixels
        return (current, drawn.astype(jnp.bfloat16))
    start = jnp.zeros((ROWS, COLS), jnp.float32)
    finished, stacked = lax.scan(advance, start, (factors, layer_keys))
    return stacked


def draw_calibration_knots(key, part):
    key_steps = jax.random.fold_in(key, 11)
    increments = jax.random.randint(key_steps, (KNOTS - 1,), 10, 1000, jnp.int32)
    tail_sums = jnp.cumsum(increments[::-1])[::-1].astype(jnp.int32)
    scaled = tail_sums * 8000 // tail_sums[0]
    knots = jnp.concatenate([scaled, jnp.zeros((1,), jnp.int32)]) + 200
    return knots.astype(jnp.int32)


def touch_ends(array, rng, low, largest):
    longest = array.shape.index(max(array.shape))
    spots = []
    for shift in (0, 1):
        where = [jax.random.randint(jax.random.fold_in(rng, axis), (), 0, length) for axis, length in enumerate(array.shape)]
        where[longest] = (where[longest] + shift) % array.shape[longest]
        spots.append(tuple(where))
    return array.at[spots[0]].set(low).at[spots[1]].set(largest)


def setup_inputs(seed: int = 0) -> dict:
    arg_keys = jax.random.split(jax.random.key(seed), 5)
    return {
        "sections": draw_sections(jax.random.fold_in(arg_keys[4], 71), 0),
        "calibration_knots": draw_calibration_knots(jax.random.fold_in(arg_keys[4], 71), 0),
        "target_offset": touch_ends(jax.random.randint(arg_keys[2], (TR, TC), 0, 64), jax.random.fold_in(arg_keys[2], 1), 0, 63).astype(jnp.int32),
        "target_step": touch_ends(jax.random.randint(arg_keys[3], (TR, TC), 32, 64), jax.random.fold_in(arg_keys[3], 1), 32, 63).astype(jnp.int32),
    }


epsilon = 1e-06

def shrink(pixels):
    leading = pixels.shape[:-2]
    row_total = pixels.shape[-2]
    col_total = pixels.shape[-1]
    blocks = pixels.astype(jnp.float32).reshape(leading + (row_total // 2, 2, col_total // 2, 2))
    return lax.optimization_barrier(jnp.mean(blocks, axis=(-3, -1))).astype(jnp.bfloat16)

def moments(current, following, row_group, half_tile):
    leading = current.shape[:-2]
    tiled_shape = leading + (current.shape[-2] // row_group, row_group, current.shape[-1] // half_tile, half_tile)
    first_tile = current.astype(jnp.float32).reshape(tiled_shape)
    second_tile = following.astype(jnp.float32).reshape(tiled_shape)

    def tile_total(values):
        return lax.optimization_barrier(jnp.sum(values, axis=(-3, -1)))
    return (tile_total(first_tile), tile_total(second_tile), tile_total(first_tile * first_tile), tile_total(second_tile * second_tile), tile_total(first_tile * second_tile))

def correlate(moment_sums, samples):
    sum_first, sum_second, sum_ff, sum_ss, sum_fs = moment_sums
    mean_first = sum_first / samples
    mean_second = sum_second / samples
    covariance = sum_fs / samples - mean_first * mean_second
    var_first = sum_ff / samples - mean_first * mean_first
    var_second = sum_ss / samples - mean_second * mean_second
    return covariance / jnp.sqrt(var_first * var_second + epsilon)

def calibrate(correlation, knot_values):
    knot_total = knot_values.shape[0]
    knot_grid = -1.0 + jnp.arange(knot_total, dtype=jnp.float32) * (2.0 / (knot_total - 1))
    hat_weights = jnp.maximum(0.0, 1.0 - jnp.abs(correlation[..., None] - knot_grid) * ((knot_total - 1) / 2.0))
    return lax.optimization_barrier(jnp.sum(hat_weights * (knot_values.astype(jnp.float32) / 1000.0), axis=-1))

def exclusive_last(values):
    running = jnp.cumsum(values, axis=-1)
    return jnp.concatenate([jnp.zeros(values.shape[:-1] + (1,), jnp.float32), running[..., :-1]], axis=-1)

def resample_weights(depths, offsets, strides, outputs):
    section_total = depths.shape[-1]
    grid_index = jnp.arange(outputs, dtype=jnp.int32)
    fraction = (offsets[..., None] + grid_index * strides[..., None]).astype(jnp.float32) / (64.0 * outputs)
    target = depths[..., -1:] * fraction
    bracket = lax.optimization_barrier(jnp.sum((depths[..., None, 1:] <= target[..., None]).astype(jnp.int32), axis=-1))
    bracket = jnp.minimum(bracket, section_total - 2)
    section_places = jnp.arange(section_total, dtype=jnp.int32)
    lower_depth = lax.optimization_barrier(jnp.sum(jnp.where(section_places == bracket[..., None], depths[..., None, :], 0.0), axis=-1))
    upper_depth = lax.optimization_barrier(jnp.sum(jnp.where(section_places == bracket[..., None] + 1, depths[..., None, :], 0.0), axis=-1))
    lifted = bracket.astype(jnp.float32) + (target - lower_depth) / (upper_depth - lower_depth)
    spread = jnp.abs(lifted[..., None] - section_places.astype(jnp.float32))
    return jnp.maximum(0.0, 1.0 - spread).astype(jnp.bfloat16)

def reference(sections, calibration_knots, target_offset, target_step):
    section_total = sections.shape[0]
    half_tile = TILE // 2
    reduced = shrink(sections)
    numerator = jnp.zeros((section_total, ROWS // TILE, COLS // TILE), jnp.float32)
    denominator = jnp.zeros((section_total, 1, 1), jnp.float32)
    for spacing in range(1, AHEAD + 1):
        forward = jnp.concatenate([reduced[spacing:], jnp.zeros((spacing,) + reduced.shape[1:], jnp.bfloat16)], axis=0)
        correlation = correlate(moments(reduced, forward, half_tile, half_tile), float(half_tile * half_tile))
        usable = (jnp.arange(section_total, dtype=jnp.int32) + spacing < section_total).astype(jnp.float32)[:, None, None]
        numerator = numerator + usable * (spacing * calibrate(correlation, calibration_knots))
        denominator = denominator + usable * float(spacing * spacing)
    thickness = numerator / jnp.maximum(denominator, 1.0)
    depths = exclusive_last(jnp.moveaxis(thickness, 0, -1))
    weights = resample_weights(depths, target_offset, target_step, NOUT)

    def one_row(inputs):
        weights_row, tile_row = inputs
        slab_pixels = lax.dynamic_slice_in_dim(sections, tile_row * TILE, TILE, 1)
        slab_pixels = slab_pixels.astype(jnp.float32).reshape(section_total, TILE, COLS // TILE, TILE)
        mixed_rows = jnp.einsum('tjs,srtc->jrtc', weights_row.astype(jnp.float32), slab_pixels, precision=lax.Precision.HIGHEST)
        return mixed_rows.reshape(NOUT, TILE, COLS).astype(jnp.bfloat16)
    per_row = lax.map(one_row, (weights, jnp.arange(ROWS // TILE, dtype=jnp.int32)))
    return jnp.transpose(per_row, (1, 0, 2, 3)).reshape(NOUT, ROWS, COLS)
```

```python
import functools

import jax
import jax.numpy as jnp
from jax import lax
from jax.experimental import pallas as pl
from jax.experimental.pallas import tpu as pltpu
from jax.sharding import PartitionSpec as P

F32 = jnp.float32
BF16 = jnp.bfloat16
MESH = pl.DeviceIdType.MESH

XS, YS, ZS = 4, 4, 8
PLANE = XS * YS
NSEC = XS * YS * ZS
ROWS = 256
COLS = 2048
TILE = 64
TILES = COLS // TILE
AHEAD = 4
KNOTS = 17
LANES = 128
BLOCKS = COLS // LANES
CHUNKS = 4
WIDE = COLS // CHUNKS
EPSILON = 1e-06
FAR = 1e9


def iota(shape, axis):
    return lax.broadcasted_iota(jnp.int32, shape, axis)


def onehot(equal):
    return jnp.where(equal, 1.0, 0.0).astype(BF16)


def dot(a, b):
    return jnp.dot(a, b, preferred_element_type=F32)


def dot_nt(a, b, precision=None):
    return lax.dot_general(
        a, b, (((1,), (1,)), ((), ())), preferred_element_type=F32, precision=precision
    )


def kernel(
    x_hbm, knots, offsets, steps, out_hbm,
    x_v, pairs, red_s, red_a, red_b, red_r, buf_a, buf_s, buf_p, weights, places,
    swap, lift_s, lift_z, lift_t, lift_y, out_v,
    in_sem, out_sem, ra_send, ra_recv, rb_send, rb_recv, a_send, a_recv, b_send, b_recv,
    lz_send, lz_recv, ly_send, ly_recv,
):
    here = lax.axis_index("sec")
    b = here // ZS
    z = here % ZS
    x = b // YS
    y = b % YS

    def plane_peer(i):
        return ((x + i // YS) % XS) * YS + (y + i % YS) % YS

    def ring_peer(i):
        return (z + i) % ZS

    load = pltpu.make_async_copy(x_hbm, x_v, in_sem)
    load.start()

    barrier = pltpu.get_barrier_semaphore()

    @pl.loop(1, PLANE)
    def _(i):
        pl.semaphore_signal(
            barrier, inc=1, device_id={"sec": plane_peer(i) * ZS + z}, device_id_type=MESH
        )

    @pl.loop(1, ZS)
    def _(i):
        pl.semaphore_signal(
            barrier, inc=1, device_id={"sec": b * ZS + ring_peer(i)}, device_id_type=MESH
        )

    def red_a_copy(i, source, target):
        return pltpu.make_async_remote_copy(
            src_ref=red_s.at[target], dst_ref=red_a.at[source],
            send_sem=ra_send.at[i], recv_sem=ra_recv.at[source],
            device_id={"sec": target * ZS + z}, device_id_type=MESH,
        )

    def red_b_copy(i, source, target):
        return pltpu.make_async_remote_copy(
            src_ref=red_b.at[target], dst_ref=red_r.at[source],
            send_sem=rb_send.at[i], recv_sem=rb_recv.at[source],
            device_id={"sec": b * ZS + target}, device_id_type=MESH,
        )

    def columns(c):
        return pl.ds(c * WIDE, WIDE)

    def rows16(i):
        return pl.ds(pl.multiple_of(i * 16, 16), 16)

    def rows32(i):
        return pl.ds(pl.multiple_of(i * 32, 32), 32)

    def a_copy(c, i, source, target):
        return pltpu.make_async_remote_copy(
            src_ref=x_hbm.at[rows16(target), columns(c)],
            dst_ref=buf_a.at[rows16(source), columns(c)],
            send_sem=a_send.at[c, i], recv_sem=a_recv.at[c, source],
            device_id={"sec": target * ZS + z}, device_id_type=MESH,
        )

    def a_own(c):
        return pltpu.make_async_copy(
            x_hbm.at[rows16(b), columns(c)], buf_a.at[rows16(b), columns(c)], a_recv.at[c, b]
        )

    def b_copy(c, i, source, target):
        return pltpu.make_async_remote_copy(
            src_ref=buf_s.at[rows32(target), columns(c)],
            dst_ref=buf_p.at[rows32(source), columns(c)],
            send_sem=b_send.at[c, i], recv_sem=b_recv.at[c, source],
            device_id={"sec": b * ZS + target}, device_id_type=MESH,
        )

    def b_own(c):
        return pltpu.make_async_copy(
            buf_s.at[rows32(z), columns(c)], buf_p.at[rows32(z), columns(c)], b_recv.at[c, z]
        )

    def lz_copy(i, source, target):
        return pltpu.make_async_remote_copy(
            src_ref=lift_s, dst_ref=lift_z.at[source],
            send_sem=lz_send.at[i], recv_sem=lz_recv.at[source],
            device_id={"sec": b * ZS + target}, device_id_type=MESH,
        )

    def ly_copy(i, source, target):
        return pltpu.make_async_remote_copy(
            src_ref=lift_t, dst_ref=lift_y.at[source],
            send_sem=ly_send.at[i], recv_sem=ly_recv.at[source],
            device_id={"sec": (x * YS + target) * ZS + z}, device_id_type=MESH,
        )

    row = iota((ROWS, ROWS), 0)
    col = iota((ROWS, ROWS), 1)
    wanted = ((row // 2) % 16) * 16 + (row // 32) * 2 + row % 2
    swap[...] = onehot(col == wanted)
    section = (((col // 2) % 16) * ZS + col // 32).astype(F32)
    places[...] = jnp.where(row % 2 == col % 2, section, FAR)

    load.wait()

    n = iota((LANES, 2 * LANES), 1)
    spread = onehot(iota((LANES, 2 * LANES), 0) // 2 == (n // LANES) * 32 + n % 32)
    quarter = iota((32, LANES), 1) // 32

    @pl.loop(0, BLOCKS)
    def _(m):
        block = x_v[:, pl.ds(pl.multiple_of(m * LANES, LANES), LANES)]
        doubled = dot(block, spread)
        halves = []
        for half in range(2):
            pairs[half] = doubled[:, half * LANES : (half + 1) * LANES]
            total = jnp.zeros((32, LANES), F32)
            for v in range(4):
                both = (
                    pairs[half, pl.ds(2 * v, 32, stride=8), :]
                    + pairs[half, pl.ds(2 * v + 1, 32, stride=8), :]
                )
                total = jnp.where(quarter == v, both, total)
            halves.append(total * 0.25)
        for tr in range(4):
            both = jnp.concatenate([h[8 * tr : 8 * tr + 8] for h in halves], axis=0)
            red_s[tr * 4 + m // 4, m % 4] = both.astype(BF16)

    pl.semaphore_wait(barrier, PLANE - 1 + ZS - 1)

    @pl.loop(1, PLANE)
    def _(i):
        red_a_copy(i, b, plane_peer(i)).start()

    own_red = pltpu.make_async_copy(red_s.at[b], red_a.at[b], ra_recv.at[b])
    own_red.start()
    for c in range(CHUNKS):
        a_own(c).start()

        @pl.loop(1, PLANE)
        def _(i):
            a_copy(c, i, b, plane_peer(i)).start()

    @pl.loop(1, PLANE)
    def _(i):
        red_a_copy(i, plane_peer(i), b).wait_recv()

    own_red.wait()
    turn = onehot(col == (row % 16) * 16 + row // 16)
    for pair in range(4):
        mixed = dot(turn, red_a[:, pair].reshape(ROWS, LANES)).astype(BF16)
        for low in range(2):
            for u in range(8):
                at = (low * 8 + u) * 16
                red_b[pair * 2 + low, :, u * LANES : (u + 1) * LANES] = mixed[at : at + 16]

    @pl.loop(1, ZS)
    def _(i):
        red_b_copy(i, z, ring_peer(i)).start()

    own_turned = pltpu.make_async_copy(red_b.at[z], red_r.at[z], rb_recv.at[z])
    own_turned.start()

    def forward(c):
        @pl.loop(1, PLANE)
        def _(i):
            a_copy(c, i, plane_peer(i), b).wait_recv()

        a_own(c).wait()
        buf_s[:, c * WIDE : (c + 1) * WIDE] = dot(
            swap[...], buf_a[:, c * WIDE : (c + 1) * WIDE]
        ).astype(BF16)

        @pl.loop(1, ZS)
        def _(i):
            b_copy(c, i, z, ring_peer(i)).start()

        b_own(c).start()

    forward(0)
    forward(1)

    @pl.loop(1, ZS)
    def _(i):
        red_b_copy(i, ring_peer(i), z).wait_recv()

    own_turned.wait()

    small_row = iota((NSEC, NSEC), 0)
    small_col = iota((NSEC, NSEC), 1)
    natural = onehot(small_col == (small_row % ZS) * PLANE + small_row // ZS)
    pixels = dot(natural, red_r[...].reshape(NSEC, 1024)).astype(BF16)
    gram = dot_nt(pixels, pixels)
    sums = dot_nt(jnp.ones((8, 1024), BF16), pixels)
    samples = 1024.0

    def diagonal(k):
        kept = jnp.where(small_row == small_col + k, gram, 0.0)
        return jnp.broadcast_to(jnp.sum(kept, axis=0, keepdims=True), (8, NSEC))

    lane = iota((8, NSEC), 1)

    def ahead(values, k):
        return jnp.where(lane < NSEC - k, pltpu.roll(values, NSEC - k, 1), 0.0)

    squares = diagonal(0)
    mean_first = sums / samples
    var_first = squares / samples - mean_first * mean_first
    knot_values = [jnp.full((8, NSEC), knots[j], jnp.int32).astype(F32) / 1000.0 for j in range(KNOTS)]
    numerator = jnp.zeros((8, NSEC), F32)
    denominator = jnp.zeros((8, NSEC), F32)
    for k in range(1, AHEAD + 1):
        mean_second = ahead(sums, k) / samples
        var_second = ahead(squares, k) / samples - mean_second * mean_second
        covariance = diagonal(k) / samples - mean_first * mean_second
        correlation = covariance / jnp.sqrt(var_first * var_second + EPSILON)
        distance = jnp.zeros((8, NSEC), F32)
        for j in range(KNOTS):
            knot = -1.0 + j * (2.0 / (KNOTS - 1))
            hat = jnp.maximum(0.0, 1.0 - jnp.abs(correlation - knot) * ((KNOTS - 1) / 2.0))
            distance = distance + hat * knot_values[j]
        usable = lane < NSEC - k
        numerator = numerator + jnp.where(usable, k * distance, 0.0)
        denominator = denominator + jnp.where(usable, float(k * k), 0.0)
    thickness = numerator / jnp.maximum(denominator, 1.0)

    def behind(values, k):
        return jnp.where(lane >= k, pltpu.roll(values, k, 1), 0.0)

    depths = behind(thickness, 1)
    reach = 1
    while reach < NSEC:
        depths = depths + behind(depths, reach)
        reach *= 2

    depth_rows = jnp.broadcast_to(depths[0:1], (NSEC, NSEC))
    depth_column = jnp.sum(jnp.where(small_row == small_col, depth_rows, 0.0), axis=1, keepdims=True)
    deepest = jnp.sum(jnp.where(lane == NSEC - 1, depths, 0.0), axis=1, keepdims=True)
    offset = offsets[x, y * ZS + z]
    stride = steps[x, y * ZS + z]
    fraction = (offset + lane * stride).astype(F32) / (64.0 * NSEC)
    target = deepest * fraction
    target_row = jnp.broadcast_to(target[0:1], (NSEC, NSEC))
    at_or_above = (depth_column <= target_row) & (small_row >= 1)
    bracket = jnp.sum(jnp.where(at_or_above, 1.0, 0.0), axis=0, keepdims=True)
    bracket = jnp.minimum(bracket, float(NSEC - 2))
    section_row = small_row.astype(F32)
    depth_full = jnp.broadcast_to(depth_column, (NSEC, NSEC))
    lower = jnp.sum(jnp.where(section_row == bracket, depth_full, 0.0), axis=0, keepdims=True)
    upper = jnp.sum(jnp.where(section_row == bracket + 1.0, depth_full, 0.0), axis=0, keepdims=True)
    lifted = bracket + (target[0:1] - lower) / (upper - lower)
    lift_s[...] = jnp.broadcast_to(lifted, (8, NSEC))

    @pl.loop(1, ZS)
    def _(i):
        lz_copy(i, z, ring_peer(i)).start()

    own_lift = pltpu.make_async_copy(lift_s, lift_z.at[z], lz_recv.at[z])
    own_lift.start()

    for c in range(2, CHUNKS):
        forward(c)

    @pl.loop(1, ZS)
    def _(i):
        lz_copy(i, ring_peer(i), z).wait_recv()

    own_lift.wait()
    eighth = iota((8, NSEC), 0)
    ring_lift = jnp.zeros((8, NSEC), F32)
    for i in range(ZS):
        ring_lift = jnp.where(eighth == i, lift_z[i], ring_lift)
    lift_t[...] = ring_lift

    @pl.loop(1, YS)
    def _(i):
        ly_copy(i, y, (y + i) % YS).start()

    own_rows = pltpu.make_async_copy(lift_t, lift_y.at[y], ly_recv.at[y])
    own_rows.start()

    @pl.loop(1, YS)
    def _(i):
        ly_copy(i, (y + i) % YS, y).wait_recv()

    own_rows.wait()

    twice = jnp.where(iota((ROWS, NSEC), 0) // 2 == iota((ROWS, NSEC), 1), 1.0, 0.0)

    @pl.loop(0, YS)
    def _(g):
        lift_columns = dot_nt(twice, lift_y[g], lax.Precision.HIGHEST)
        for i in range(ZS):
            apart = jnp.abs(lift_columns[:, i : i + 1] - places[...])
            weights[g * ZS + i] = jnp.maximum(0.0, 1.0 - apart).astype(BF16)

    left = iota((ROWS, LANES), 1) < TILE

    def out_copy(c):
        return pltpu.make_async_copy(
            out_v.at[:, columns(c)], out_hbm.at[:, columns(c)], out_sem.at[c]
        )

    for c in range(CHUNKS):

        @pl.loop(1, ZS)
        def _(i):
            b_copy(c, i, ring_peer(i), z).wait_recv()

        b_own(c).wait()

        @pl.loop(c * (WIDE // LANES), (c + 1) * (WIDE // LANES))
        def _(m):
            at = pl.ds(pl.multiple_of(m * LANES, LANES), LANES)
            block = buf_p[:, at]
            first = dot(weights[2 * m], block)
            second = dot(weights[2 * m + 1], block)
            out_v[:, at] = jnp.where(left, first, second).astype(BF16)

        out_copy(c).start()

    for c in range(CHUNKS):
        out_copy(c).wait()

    @pl.loop(1, PLANE)
    def _(i):
        red_a_copy(i, b, plane_peer(i)).wait_send()
        for c in range(CHUNKS):
            a_copy(c, i, b, plane_peer(i)).wait_send()

    @pl.loop(1, ZS)
    def _(i):
        red_b_copy(i, z, ring_peer(i)).wait_send()
        lz_copy(i, z, ring_peer(i)).wait_send()
        for c in range(CHUNKS):
            b_copy(c, i, z, ring_peer(i)).wait_send()

    @pl.loop(1, YS)
    def _(i):
        ly_copy(i, y, (y + i) % YS).wait_send()


def per_device(sections, calibration_knots, target_offset, target_step):
    dma = pltpu.SemaphoreType.DMA
    out = pl.pallas_call(
        kernel,
        out_shape=jax.ShapeDtypeStruct((ROWS, COLS), BF16),
        in_specs=[pl.BlockSpec(memory_space=pl.ANY)]
        + [pl.BlockSpec(memory_space=pltpu.SMEM)] * 3,
        out_specs=pl.BlockSpec(memory_space=pl.ANY),
        scratch_shapes=[
            pltpu.VMEM((ROWS, COLS), BF16),
            pltpu.VMEM((2, ROWS, LANES), F32),
            pltpu.VMEM((PLANE, 4, 16, LANES), BF16),
            pltpu.VMEM((PLANE, 4, 16, LANES), BF16),
            pltpu.VMEM((ZS, PLANE, 1024), BF16),
            pltpu.VMEM((ZS, PLANE, 1024), BF16),
            pltpu.VMEM((ROWS, COLS), BF16),
            pltpu.VMEM((ROWS, COLS), BF16),
            pltpu.VMEM((ROWS, COLS), BF16),
            pltpu.VMEM((TILES, ROWS, ROWS), BF16),
            pltpu.VMEM((ROWS, ROWS), F32),
            pltpu.VMEM((ROWS, ROWS), BF16),
            pltpu.VMEM((8, NSEC), F32),
            pltpu.VMEM((ZS, 8, NSEC), F32),
            pltpu.VMEM((8, NSEC), F32),
            pltpu.VMEM((YS, 8, NSEC), F32),
            pltpu.VMEM((ROWS, COLS), BF16),
            dma, dma((CHUNKS,)), dma((PLANE,)), dma((PLANE,)), dma((ZS,)), dma((ZS,)),
            dma((CHUNKS, PLANE)), dma((CHUNKS, PLANE)), dma((CHUNKS, ZS)), dma((CHUNKS, ZS)),
            dma((ZS,)), dma((ZS,)), dma((YS,)), dma((YS,)),
        ],
        compiler_params=pltpu.CompilerParams(collective_id=0, has_side_effects=True),
    )(sections.reshape(ROWS, COLS), calibration_knots, target_offset, target_step)
    return out.reshape(NSEC, 2, COLS)


def solution(mesh):
    return jax.shard_map(
        per_device,
        mesh=mesh,
        in_specs=(P("sec", None, "tile"), P(), P(None, "tile"), P(None, "tile")),
        out_specs=P(None, "sec", "tile"),
        check_vma=False,
    )
```

```python
import functools

import jax
import jax.numpy as jnp
from jax import lax
from jax.experimental import pallas as pl
from jax.experimental.pallas import tpu as pltpu
from jax.sharding import PartitionSpec as P

F32 = jnp.float32
BF16 = jnp.bfloat16
MESH = pl.DeviceIdType.MESH

XS, YS, ZS = 4, 4, 8
PLANE = XS * YS
NSEC = XS * YS * ZS
ROWS = 256
COLS = 2048
TILE = 64
TILES = COLS // TILE
AHEAD = 4
KNOTS = 17
LANES = 128
BLOCKS = COLS // LANES
FIRST = 512
WIDE = 256
CHUNKS = (COLS - FIRST) // WIDE
AHEAD_CHUNKS = 2
EPSILON = 1e-06
FAR = 1e9


def iota(shape, axis):
    return lax.broadcasted_iota(jnp.int32, shape, axis)


def onehot(equal):
    return jnp.where(equal, 1.0, 0.0).astype(BF16)


def dot(a, b):
    return jnp.dot(a, b, preferred_element_type=F32)


def dot_nt(a, b, precision=None):
    return lax.dot_general(
        a, b, (((1,), (1,)), ((), ())), preferred_element_type=F32, precision=precision
    )


def kernel(
    x_hbm, knots_hbm, offsets_hbm, steps_hbm, out_hbm,
    x_v, pairs, red_s, red_a, red_b, red_r, buf_a, buf_s, buf_p, weights, places, places_first,
    swap, unswap, lift_s, lift_z, lift_t, lift_y, out_v,
    knots, offsets, steps, in_sem, out_sem, sent, came, a_came, b_came,
):
    here = lax.axis_index("sec")
    b = here // ZS
    z = here % ZS
    x = b // YS
    y = b % YS

    def plane_peer(i):
        return ((x + i // YS) % XS) * YS + (y + i % YS) % YS

    def ring_peer(i):
        return (z + i) % ZS

    head = pl.ds(0, FIRST)
    tail = pl.ds(FIRST, COLS - FIRST)
    load_head = pltpu.make_async_copy(x_hbm.at[:, head], x_v.at[:, head], in_sem.at[0])
    load_tail = pltpu.make_async_copy(x_hbm.at[:, tail], x_v.at[:, tail], in_sem.at[1])
    load_head.start()
    load_tail.start()
    small = [
        pltpu.make_async_copy(source, target, in_sem.at[2 + i])
        for i, (source, target) in enumerate(
            ((knots_hbm, knots), (offsets_hbm, offsets), (steps_hbm, steps))
        )
    ]
    for copy in small:
        copy.start()

    barrier = pltpu.get_barrier_semaphore()

    @pl.loop(1, PLANE)
    def _(i):
        pl.semaphore_signal(
            barrier, inc=1, device_id={"sec": plane_peer(i) * ZS + z}, device_id_type=MESH
        )

    @pl.loop(1, ZS)
    def _(i):
        pl.semaphore_signal(
            barrier, inc=1, device_id={"sec": b * ZS + ring_peer(i)}, device_id_type=MESH
        )

    def arrived(region, semaphore):
        pltpu.make_async_copy(region, region, semaphore).wait()

    def red_a_copy(i, source, target):
        return pltpu.make_async_remote_copy(
            src_ref=red_s.at[target], dst_ref=red_a.at[source],
            send_sem=sent.at[0], recv_sem=came.at[0],
            device_id={"sec": target * ZS + z}, device_id_type=MESH,
        )

    def red_b_copy(i, source, target):
        return pltpu.make_async_remote_copy(
            src_ref=red_b.at[target], dst_ref=red_r.at[source],
            send_sem=sent.at[1], recv_sem=came.at[1],
            device_id={"sec": b * ZS + target}, device_id_type=MESH,
        )

    def columns(c):
        return pl.ds(FIRST + c * WIDE, WIDE)

    def rows16(i):
        return pl.ds(pl.multiple_of(i * 16, 16), 16)

    def rows32(i):
        return pl.ds(pl.multiple_of(i * 32, 32), 32)

    def a_copy(c, i, source, target):
        return pltpu.make_async_remote_copy(
            src_ref=x_hbm.at[rows16(target), columns(c)],
            dst_ref=buf_a.at[rows16(source), columns(c)],
            send_sem=sent.at[6], recv_sem=a_came.at[c],
            device_id={"sec": target * ZS + z}, device_id_type=MESH,
        )

    def a_own(c):
        return pltpu.make_async_copy(
            x_hbm.at[rows16(b), columns(c)], buf_a.at[rows16(b), columns(c)], a_came.at[c]
        )

    def b_copy(c, i, source, target):
        return pltpu.make_async_remote_copy(
            src_ref=buf_s.at[rows32(target), columns(c)],
            dst_ref=buf_p.at[rows32(source), columns(c)],
            send_sem=sent.at[7], recv_sem=b_came.at[c],
            device_id={"sec": b * ZS + target}, device_id_type=MESH,
        )

    def b_own(c):
        return pltpu.make_async_copy(
            buf_s.at[rows32(z), columns(c)], buf_p.at[rows32(z), columns(c)], b_came.at[c]
        )

    def zf_copy(i, source, target):
        return pltpu.make_async_remote_copy(
            src_ref=buf_s.at[rows32(target), head], dst_ref=buf_a.at[rows32(source), head],
            send_sem=sent.at[4], recv_sem=came.at[4],
            device_id={"sec": b * ZS + target}, device_id_type=MESH,
        )

    def pf_copy(i, source, target):
        return pltpu.make_async_remote_copy(
            src_ref=x_v.at[rows16(target), head], dst_ref=buf_p.at[rows16(source), head],
            send_sem=sent.at[5], recv_sem=came.at[5],
            device_id={"sec": target * ZS + z}, device_id_type=MESH,
        )

    def lz_copy(i, source, target):
        return pltpu.make_async_remote_copy(
            src_ref=lift_s, dst_ref=lift_z.at[source],
            send_sem=sent.at[2], recv_sem=came.at[2],
            device_id={"sec": b * ZS + target}, device_id_type=MESH,
        )

    def ly_copy(i, source, target):
        return pltpu.make_async_remote_copy(
            src_ref=lift_t, dst_ref=lift_y.at[source],
            send_sem=sent.at[3], recv_sem=came.at[3],
            device_id={"sec": (x * YS + target) * ZS + z}, device_id_type=MESH,
        )

    row = iota((ROWS, ROWS), 0)
    col = iota((ROWS, ROWS), 1)
    wanted = ((row // 2) % 16) * 16 + (row // 32) * 2 + row % 2
    swap[...] = onehot(col == wanted)
    section = (((col // 2) % 16) * ZS + col // 32).astype(F32)
    places[...] = jnp.where(row % 2 == col % 2, section, FAR)
    places_first[...] = jnp.where(row % 2 == col % 2, (col // 2).astype(F32), FAR)
    unswap[...] = onehot(col == ((row // 2) % ZS) * 32 + (row // 16) * 2 + row % 2)

    load_head.wait()
    buf_s[:, :FIRST] = dot(swap[...], x_v[:, :FIRST]).astype(BF16)

    pl.semaphore_wait(barrier, PLANE - 1 + ZS - 1)

    @pl.loop(1, ZS)
    def _(i):
        zf_copy(i, z, ring_peer(i)).start()

    own_first = pltpu.make_async_copy(
        buf_s.at[rows32(z), head], buf_a.at[rows32(z), head], came.at[4]
    )
    own_first.start()

    def outward(c):
        a_own(c).start()

        @pl.loop(1, PLANE)
        def _(i):
            a_copy(c, i, b, plane_peer(i)).start()

    for c in range(AHEAD_CHUNKS):
        outward(c)

    load_tail.wait()

    n = iota((LANES, 2 * LANES), 1)
    spread = onehot(iota((LANES, 2 * LANES), 0) // 2 == (n // LANES) * 32 + n % 32)
    quarter = iota((32, LANES), 1) // 32

    @pl.loop(0, BLOCKS)
    def _(m):
        block = x_v[:, pl.ds(pl.multiple_of(m * LANES, LANES), LANES)]
        doubled = dot(block, spread)
        halves = []
        for half in range(2):
            pairs[half] = doubled[:, half * LANES : (half + 1) * LANES]
            total = jnp.zeros((32, LANES), F32)
            for v in range(4):
                both = (
                    pairs[half, pl.ds(2 * v, 32, stride=8), :]
                    + pairs[half, pl.ds(2 * v + 1, 32, stride=8), :]
                )
                total = jnp.where(quarter == v, both, total)
            halves.append(total * 0.25)
        for tr in range(4):
            both = jnp.concatenate([h[8 * tr : 8 * tr + 8] for h in halves], axis=0)
            red_s[tr * 4 + m // 4, m % 4] = both.astype(BF16)

    @pl.loop(1, PLANE)
    def _(i):
        red_a_copy(i, b, plane_peer(i)).start()

    own_red = pltpu.make_async_copy(red_s.at[b], red_a.at[b], came.at[0])
    own_red.start()
    def forward(c):
        arrived(buf_a.at[:, columns(c)], a_came.at[c])
        buf_s[:, columns(c)] = dot(swap[...], buf_a[:, columns(c)]).astype(BF16)

        @pl.loop(1, ZS)
        def _(i):
            b_copy(c, i, z, ring_peer(i)).start()

        b_own(c).start()
        if c + AHEAD_CHUNKS < CHUNKS:
            outward(c + AHEAD_CHUNKS)

    forward(0)

    arrived(red_a, came.at[0])
    turn = onehot(col == (row % 16) * 16 + row // 16)
    for pair in range(4):
        mixed = dot(turn, red_a[:, pair].reshape(ROWS, LANES)).astype(BF16)
        for low in range(2):
            for u in range(8):
                at = (low * 8 + u) * 16
                red_b[pair * 2 + low, :, u * LANES : (u + 1) * LANES] = mixed[at : at + 16]

    @pl.loop(1, ZS)
    def _(i):
        red_b_copy(i, z, ring_peer(i)).start()

    own_turned = pltpu.make_async_copy(red_b.at[z], red_r.at[z], came.at[1])
    own_turned.start()

    forward(1)

    arrived(buf_a.at[:, head], came.at[4])
    x_v[:, :FIRST] = dot(unswap[...], buf_a[:, :FIRST]).astype(BF16)

    @pl.loop(1, PLANE)
    def _(i):
        pf_copy(i, b, plane_peer(i)).start()

    own_crossed = pltpu.make_async_copy(
        x_v.at[rows16(b), head], buf_p.at[rows16(b), head], came.at[5]
    )
    own_crossed.start()
    forward(2)

    arrived(red_r, came.at[1])
    for copy in small:
        copy.wait()

    small_row = iota((NSEC, NSEC), 0)
    small_col = iota((NSEC, NSEC), 1)
    natural = onehot(small_col == (small_row % ZS) * PLANE + small_row // ZS)
    pixels = dot(natural, red_r[...].reshape(NSEC, 1024)).astype(BF16)
    gram = dot_nt(pixels, pixels)
    sums = dot_nt(jnp.ones((8, 1024), BF16), pixels)
    samples = 1024.0

    def diagonal(k):
        kept = jnp.where(small_row == small_col + k, gram, 0.0)
        return jnp.broadcast_to(jnp.sum(kept, axis=0, keepdims=True), (8, NSEC))

    lane = iota((8, NSEC), 1)

    def ahead(values, k):
        return jnp.where(lane < NSEC - k, pltpu.roll(values, NSEC - k, 1), 0.0)

    squares = diagonal(0)
    mean_first = sums / samples
    var_first = squares / samples - mean_first * mean_first
    knot_values = [jnp.full((8, NSEC), knots[j], jnp.int32).astype(F32) / 1000.0 for j in range(KNOTS)]
    numerator = jnp.zeros((8, NSEC), F32)
    denominator = jnp.zeros((8, NSEC), F32)
    for k in range(1, AHEAD + 1):
        mean_second = ahead(sums, k) / samples
        var_second = ahead(squares, k) / samples - mean_second * mean_second
        covariance = diagonal(k) / samples - mean_first * mean_second
        correlation = covariance / jnp.sqrt(var_first * var_second + EPSILON)
        distance = jnp.zeros((8, NSEC), F32)
        for j in range(KNOTS):
            knot = -1.0 + j * (2.0 / (KNOTS - 1))
            hat = jnp.maximum(0.0, 1.0 - jnp.abs(correlation - knot) * ((KNOTS - 1) / 2.0))
            distance = distance + hat * knot_values[j]
        usable = lane < NSEC - k
        numerator = numerator + jnp.where(usable, k * distance, 0.0)
        denominator = denominator + jnp.where(usable, float(k * k), 0.0)
    thickness = numerator / jnp.maximum(denominator, 1.0)

    def behind(values, k):
        return jnp.where(lane >= k, pltpu.roll(values, k, 1), 0.0)

    depths = behind(thickness, 1)
    reach = 1
    while reach < NSEC:
        depths = depths + behind(depths, reach)
        reach *= 2

    depth_rows = jnp.broadcast_to(depths[0:1], (NSEC, NSEC))
    depth_column = jnp.sum(jnp.where(small_row == small_col, depth_rows, 0.0), axis=1, keepdims=True)
    deepest = jnp.sum(jnp.where(lane == NSEC - 1, depths, 0.0), axis=1, keepdims=True)
    offset = offsets[x, y * ZS + z]
    stride = steps[x, y * ZS + z]
    fraction = (offset + lane * stride).astype(F32) / (64.0 * NSEC)
    target = deepest * fraction
    target_row = jnp.broadcast_to(target[0:1], (NSEC, NSEC))
    at_or_above = (depth_column <= target_row) & (small_row >= 1)
    bracket = jnp.sum(jnp.where(at_or_above, 1.0, 0.0), axis=0, keepdims=True)
    bracket = jnp.minimum(bracket, float(NSEC - 2))
    section_row = small_row.astype(F32)
    depth_full = jnp.broadcast_to(depth_column, (NSEC, NSEC))
    lower = jnp.sum(jnp.where(section_row == bracket, depth_full, 0.0), axis=0, keepdims=True)
    upper = jnp.sum(jnp.where(section_row == bracket + 1.0, depth_full, 0.0), axis=0, keepdims=True)
    lifted = bracket + (target[0:1] - lower) / (upper - lower)
    lift_s[...] = jnp.broadcast_to(lifted, (8, NSEC))

    @pl.loop(1, ZS)
    def _(i):
        lz_copy(i, z, ring_peer(i)).start()

    own_lift = pltpu.make_async_copy(lift_s, lift_z.at[z], came.at[2])
    own_lift.start()

    for c in range(3, CHUNKS - 1):
        forward(c)

    arrived(lift_z, came.at[2])
    eighth = iota((8, NSEC), 0)
    ring_lift = jnp.zeros((8, NSEC), F32)
    for i in range(ZS):
        ring_lift = jnp.where(eighth == i, lift_z[i], ring_lift)
    lift_t[...] = ring_lift

    @pl.loop(1, YS)
    def _(i):
        ly_copy(i, y, (y + i) % YS).start()

    own_rows = pltpu.make_async_copy(lift_t, lift_y.at[y], came.at[3])
    own_rows.start()
    forward(CHUNKS - 1)

    arrived(lift_y, came.at[3])

    twice = jnp.where(iota((ROWS, NSEC), 0) // 2 == iota((ROWS, NSEC), 1), 1.0, 0.0)

    def weigh(where):
        def group(g):
            lift_columns = dot_nt(twice, lift_y[g], lax.Precision.HIGHEST)
            for i in range(ZS):
                apart = jnp.abs(lift_columns[:, i : i + 1] - where[...])
                weights[g * ZS + i] = jnp.maximum(0.0, 1.0 - apart).astype(BF16)

        return group

    pl.loop(0, FIRST // TILE // ZS)(weigh(places_first))
    pl.loop(FIRST // TILE // ZS, YS)(weigh(places))

    left = iota((ROWS, LANES), 1) < TILE

    def out_copy(at):
        return pltpu.make_async_copy(out_v.at[:, at], out_hbm.at[:, at], out_sem)

    def mix(low, high):
        @pl.loop(low // LANES, high // LANES)
        def _(m):
            at = pl.ds(pl.multiple_of(m * LANES, LANES), LANES)
            block = buf_p[:, at]
            first = dot(weights[2 * m], block)
            second = dot(weights[2 * m + 1], block)
            out_v[:, at] = jnp.where(left, first, second).astype(BF16)

    arrived(buf_p.at[:, head], came.at[5])
    mix(0, FIRST)
    out_copy(head).start()

    for c in range(CHUNKS):
        arrived(buf_p.at[:, columns(c)], b_came.at[c])
        mix(FIRST + c * WIDE, FIRST + (c + 1) * WIDE)
        out_copy(columns(c)).start()

    arrived(out_v, out_sem)

    for n, region in enumerate(
        (
            red_a.at[: PLANE - 1],
            red_r.at[: ZS - 1],
            lift_z.at[: ZS - 1],
            lift_y.at[: YS - 1],
            buf_a.at[: ROWS - 32, head],
            buf_p.at[: ROWS - 16, head],
            buf_a.at[: ROWS - 16, tail],
            buf_s.at[: ROWS - 32, tail],
        )
    ):
        arrived(region, sent.at[n])


def per_device(sections, calibration_knots, target_offset, target_step):
    dma = pltpu.SemaphoreType.DMA
    out = pl.pallas_call(
        kernel,
        out_shape=jax.ShapeDtypeStruct((ROWS, COLS), BF16),
        in_specs=[pl.BlockSpec(memory_space=pl.ANY)]
        + [pl.BlockSpec(memory_space=pl.ANY)] * 3,
        out_specs=pl.BlockSpec(memory_space=pl.ANY),
        scratch_shapes=[
            pltpu.VMEM((ROWS, COLS), BF16),
            pltpu.VMEM((2, ROWS, LANES), F32),
            pltpu.VMEM((PLANE, 4, 16, LANES), BF16),
            pltpu.VMEM((PLANE, 4, 16, LANES), BF16),
            pltpu.VMEM((ZS, PLANE, 1024), BF16),
            pltpu.VMEM((ZS, PLANE, 1024), BF16),
            pltpu.VMEM((ROWS, COLS), BF16),
            pltpu.VMEM((ROWS, COLS), BF16),
            pltpu.VMEM((ROWS, COLS), BF16),
            pltpu.VMEM((TILES, ROWS, ROWS), BF16),
            pltpu.VMEM((ROWS, ROWS), F32),
            pltpu.VMEM((ROWS, ROWS), F32),
            pltpu.VMEM((ROWS, ROWS), BF16),
            pltpu.VMEM((ROWS, ROWS), BF16),
            pltpu.VMEM((8, NSEC), F32),
            pltpu.VMEM((ZS, 8, NSEC), F32),
            pltpu.VMEM((8, NSEC), F32),
            pltpu.VMEM((YS, 8, NSEC), F32),
            pltpu.VMEM((ROWS, COLS), BF16),
            pltpu.SMEM((KNOTS,), jnp.int32),
            pltpu.SMEM((4, TILES), jnp.int32),
            pltpu.SMEM((4, TILES), jnp.int32),
            dma((5,)), dma, dma((8,)), dma((6,)), dma((CHUNKS,)), dma((CHUNKS,)),
        ],
        compiler_params=pltpu.CompilerParams(collective_id=0, has_side_effects=True),
    )(sections.reshape(ROWS, COLS), calibration_knots, target_offset, target_step)
    return out.reshape(NSEC, 2, COLS)


def solution(mesh):
    return jax.shard_map(
        per_device,
        mesh=mesh,
        in_specs=(P("sec", None, "tile"), P(), P(None, "tile"), P(None, "tile")),
        out_specs=P(None, "sec", "tile"),
        check_vma=False,
    )
```

```python
import functools

import jax
import jax.numpy as jnp
from jax import lax
from jax.experimental import pallas as pl
from jax.experimental.pallas import tpu as pltpu
from jax.sharding import PartitionSpec as P

F32 = jnp.float32
BF16 = jnp.bfloat16
MESH = pl.DeviceIdType.MESH

XS, YS, ZS = 4, 4, 8
PLANE = XS * YS
NSEC = XS * YS * ZS
ROWS = 256
COLS = 2048
TILE = 64
TILES = COLS // TILE
AHEAD = 4
KNOTS = 17
LANES = 128
BLOCKS = COLS // LANES
FIRST = 512
WIDTHS = (384, 256, 256, 256, 256, 128)
CHUNKS = len(WIDTHS)
STARTS = tuple(FIRST + sum(WIDTHS[:c]) for c in range(CHUNKS + 1))
PLAN = (
    "h r b z A o0 o1 t f0 o2 p o3 g f1 o4 f2 o5 y f3 f4 f5 w m M0 M1 M2 M3 M4 M5"
)
EPSILON = 1e-06
FAR = 1e9


def iota(shape, axis):
    return lax.broadcasted_iota(jnp.int32, shape, axis)


def onehot(equal):
    return jnp.where(equal, 1.0, 0.0).astype(BF16)


def dot(a, b):
    return jnp.dot(a, b, preferred_element_type=F32)


def dot_nt(a, b, precision=None):
    return lax.dot_general(
        a, b, (((1,), (1,)), ((), ())), preferred_element_type=F32, precision=precision
    )


def kernel(
    x_hbm, knots_hbm, offsets_hbm, steps_hbm, out_v,
    x_v, pairs, red_s, red_a, red_b, red_r, buf_a, buf_s, buf_p, weights, places, places_first,
    swap, unswap, lift_s, lift_z, lift_t, lift_y,
    knots, offsets, steps, in_sem, sent, came, a_came, b_came,
):
    here = lax.axis_index("sec")
    b = here // ZS
    z = here % ZS
    x = b // YS
    y = b % YS

    def plane_peer(i):
        return ((x + i // YS) % XS) * YS + (y + i % YS) % YS

    def ring_peer(i):
        return (z + i) % ZS

    head = pl.ds(0, FIRST)
    tail = pl.ds(FIRST, COLS - FIRST)
    load_head = pltpu.make_async_copy(x_hbm.at[:, head], x_v.at[:, head], in_sem.at[0])
    load_tail = pltpu.make_async_copy(x_hbm.at[:, tail], x_v.at[:, tail], in_sem.at[1])
    load_head.start()
    load_tail.start()
    small = [
        pltpu.make_async_copy(source, target, in_sem.at[2 + i])
        for i, (source, target) in enumerate(
            ((knots_hbm, knots), (offsets_hbm, offsets), (steps_hbm, steps))
        )
    ]
    for copy in small:
        copy.start()

    barrier = pltpu.get_barrier_semaphore()

    @pl.loop(1, PLANE)
    def _(i):
        pl.semaphore_signal(
            barrier, inc=1, device_id={"sec": plane_peer(i) * ZS + z}, device_id_type=MESH
        )

    @pl.loop(1, ZS)
    def _(i):
        pl.semaphore_signal(
            barrier, inc=1, device_id={"sec": b * ZS + ring_peer(i)}, device_id_type=MESH
        )

    def arrived(region, semaphore):
        pltpu.make_async_copy(region, region, semaphore).wait()

    def red_a_copy(i, source, target):
        return pltpu.make_async_remote_copy(
            src_ref=red_s.at[target], dst_ref=red_a.at[source],
            send_sem=sent.at[0], recv_sem=came.at[0],
            device_id={"sec": target * ZS + z}, device_id_type=MESH,
        )

    def red_b_copy(i, source, target):
        return pltpu.make_async_remote_copy(
            src_ref=red_b.at[target], dst_ref=red_r.at[source],
            send_sem=sent.at[1], recv_sem=came.at[1],
            device_id={"sec": b * ZS + target}, device_id_type=MESH,
        )

    def columns(c):
        return pl.ds(STARTS[c], WIDTHS[c])

    def rows16(i):
        return pl.ds(pl.multiple_of(i * 16, 16), 16)

    def rows32(i):
        return pl.ds(pl.multiple_of(i * 32, 32), 32)

    def a_copy(c, i, source, target):
        return pltpu.make_async_remote_copy(
            src_ref=x_hbm.at[rows16(target), columns(c)],
            dst_ref=buf_a.at[rows16(source), columns(c)],
            send_sem=sent.at[6], recv_sem=a_came.at[c],
            device_id={"sec": target * ZS + z}, device_id_type=MESH,
        )

    def a_own(c):
        return pltpu.make_async_copy(
            x_hbm.at[rows16(b), columns(c)], buf_a.at[rows16(b), columns(c)], a_came.at[c]
        )

    def b_copy(c, i, source, target):
        return pltpu.make_async_remote_copy(
            src_ref=buf_s.at[rows32(target), columns(c)],
            dst_ref=buf_p.at[rows32(source), columns(c)],
            send_sem=sent.at[7], recv_sem=b_came.at[c],
            device_id={"sec": b * ZS + target}, device_id_type=MESH,
        )

    def b_own(c):
        return pltpu.make_async_copy(
            buf_s.at[rows32(z), columns(c)], buf_p.at[rows32(z), columns(c)], b_came.at[c]
        )

    def zf_copy(i, source, target):
        return pltpu.make_async_remote_copy(
            src_ref=buf_s.at[rows32(target), head], dst_ref=buf_a.at[rows32(source), head],
            send_sem=sent.at[4], recv_sem=came.at[4],
            device_id={"sec": b * ZS + target}, device_id_type=MESH,
        )

    def pf_copy(i, source, target):
        return pltpu.make_async_remote_copy(
            src_ref=x_v.at[rows16(target), head], dst_ref=buf_p.at[rows16(source), head],
            send_sem=sent.at[5], recv_sem=came.at[5],
            device_id={"sec": target * ZS + z}, device_id_type=MESH,
        )

    def lz_copy(i, source, target):
        return pltpu.make_async_remote_copy(
            src_ref=lift_s, dst_ref=lift_z.at[source],
            send_sem=sent.at[2], recv_sem=came.at[2],
            device_id={"sec": b * ZS + target}, device_id_type=MESH,
        )

    def ly_copy(i, source, target):
        return pltpu.make_async_remote_copy(
            src_ref=lift_t, dst_ref=lift_y.at[source],
            send_sem=sent.at[3], recv_sem=came.at[3],
            device_id={"sec": (x * YS + target) * ZS + z}, device_id_type=MESH,
        )

    row = iota((ROWS, ROWS), 0)
    col = iota((ROWS, ROWS), 1)
    wanted = ((row // 2) % 16) * 16 + (row // 32) * 2 + row % 2
    swap[...] = onehot(col == wanted)
    section = (((col // 2) % 16) * ZS + col // 32).astype(F32)
    places[...] = jnp.where(row % 2 == col % 2, section, FAR)
    places_first[...] = jnp.where(row % 2 == col % 2, (col // 2).astype(F32), FAR)
    unswap[...] = onehot(col == ((row // 2) % ZS) * 32 + (row // 16) * 2 + row % 2)

    def turn_first():
        load_head.wait()
        buf_s[:, :FIRST] = dot(swap[...], x_v[:, :FIRST]).astype(BF16)

    def meet():
        pl.semaphore_wait(barrier, PLANE - 1 + ZS - 1)

    def to_ring(copy, own):
        @pl.loop(1, ZS)
        def _(i):
            copy(i, z, ring_peer(i)).start()

        own.start()

    def to_plane(copy, own):
        @pl.loop(1, PLANE)
        def _(i):
            copy(i, b, plane_peer(i)).start()

        own.start()

    def first_round_ring():
        to_ring(
            zf_copy,
            pltpu.make_async_copy(
                buf_s.at[rows32(z), head], buf_a.at[rows32(z), head], came.at[4]
            ),
        )

    def outward(c):
        to_plane(functools.partial(a_copy, c), a_own(c))

    def forward(c):
        arrived(buf_a.at[:, columns(c)], a_came.at[c])
        buf_s[:, columns(c)] = dot(swap[...], buf_a[:, columns(c)]).astype(BF16)
        to_ring(functools.partial(b_copy, c), b_own(c))

    def reduce():
        load_tail.wait()
        n = iota((LANES, 2 * LANES), 1)
        spread = onehot(iota((LANES, 2 * LANES), 0) // 2 == (n // LANES) * 32 + n % 32)
        quarter = iota((32, LANES), 1) // 32

        @pl.loop(0, BLOCKS)
        def _(m):
            block = x_v[:, pl.ds(pl.multiple_of(m * LANES, LANES), LANES)]
            doubled = dot(block, spread)
            halves = []
            for half in range(2):
                pairs[half] = doubled[:, half * LANES : (half + 1) * LANES]
                total = jnp.zeros((32, LANES), F32)
                for v in range(4):
                    both = (
                        pairs[half, pl.ds(2 * v, 32, stride=8), :]
                        + pairs[half, pl.ds(2 * v + 1, 32, stride=8), :]
                    )
                    total = jnp.where(quarter == v, both, total)
                halves.append(total * 0.25)
            for tr in range(4):
                both = jnp.concatenate([h[8 * tr : 8 * tr + 8] for h in halves], axis=0)
                red_s[tr * 4 + m // 4, m % 4] = both.astype(BF16)
    def spread_reduced():
        to_plane(red_a_copy, pltpu.make_async_copy(red_s.at[b], red_a.at[b], came.at[0]))

    def turn_reduced():
        arrived(red_a, came.at[0])
        turn = onehot(col == (row % 16) * 16 + row // 16)
        for pair in range(4):
            mixed = dot(turn, red_a[:, pair].reshape(ROWS, LANES)).astype(BF16)
            for low in range(2):
                for u in range(8):
                    at = (low * 8 + u) * 16
                    red_b[pair * 2 + low, :, u * LANES : (u + 1) * LANES] = mixed[at : at + 16]
        to_ring(red_b_copy, pltpu.make_async_copy(red_b.at[z], red_r.at[z], came.at[1]))

    def lift_tile():
        arrived(red_r, came.at[1])
        for copy in small:
            copy.wait()

        small_row = iota((NSEC, NSEC), 0)
        small_col = iota((NSEC, NSEC), 1)
        natural = onehot(small_col == (small_row % ZS) * PLANE + small_row // ZS)
        pixels = dot(natural, red_r[...].reshape(NSEC, 1024)).astype(BF16)
        gram = dot_nt(pixels, pixels)
        sums = dot_nt(jnp.ones((8, 1024), BF16), pixels)
        samples = 1024.0

        def diagonal(k):
            kept = jnp.where(small_row == small_col + k, gram, 0.0)
            return jnp.broadcast_to(jnp.sum(kept, axis=0, keepdims=True), (8, NSEC))

        lane = iota((8, NSEC), 1)

        def ahead(values, k):
            return jnp.where(lane < NSEC - k, pltpu.roll(values, NSEC - k, 1), 0.0)

        squares = diagonal(0)
        mean_first = sums / samples
        var_first = squares / samples - mean_first * mean_first
        knot_values = [jnp.full((8, NSEC), knots[j], jnp.int32).astype(F32) / 1000.0 for j in range(KNOTS)]
        numerator = jnp.zeros((8, NSEC), F32)
        denominator = jnp.zeros((8, NSEC), F32)
        for k in range(1, AHEAD + 1):
            mean_second = ahead(sums, k) / samples
            var_second = ahead(squares, k) / samples - mean_second * mean_second
            covariance = diagonal(k) / samples - mean_first * mean_second
            correlation = covariance / jnp.sqrt(var_first * var_second + EPSILON)
            distance = jnp.zeros((8, NSEC), F32)
            for j in range(KNOTS):
                knot = -1.0 + j * (2.0 / (KNOTS - 1))
                hat = jnp.maximum(0.0, 1.0 - jnp.abs(correlation - knot) * ((KNOTS - 1) / 2.0))
                distance = distance + hat * knot_values[j]
            usable = lane < NSEC - k
            numerator = numerator + jnp.where(usable, k * distance, 0.0)
            denominator = denominator + jnp.where(usable, float(k * k), 0.0)
        thickness = numerator / jnp.maximum(denominator, 1.0)

        def behind(values, k):
            return jnp.where(lane >= k, pltpu.roll(values, k, 1), 0.0)

        depths = behind(thickness, 1)
        reach = 1
        while reach < NSEC:
            depths = depths + behind(depths, reach)
            reach *= 2

        depth_rows = jnp.broadcast_to(depths[0:1], (NSEC, NSEC))
        depth_column = jnp.sum(jnp.where(small_row == small_col, depth_rows, 0.0), axis=1, keepdims=True)
        deepest = jnp.sum(jnp.where(lane == NSEC - 1, depths, 0.0), axis=1, keepdims=True)
        offset = offsets[x, y * ZS + z]
        stride = steps[x, y * ZS + z]
        fraction = (offset + lane * stride).astype(F32) / (64.0 * NSEC)
        target = deepest * fraction
        target_row = jnp.broadcast_to(target[0:1], (NSEC, NSEC))
        at_or_above = (depth_column <= target_row) & (small_row >= 1)
        bracket = jnp.sum(jnp.where(at_or_above, 1.0, 0.0), axis=0, keepdims=True)
        bracket = jnp.minimum(bracket, float(NSEC - 2))
        section_row = small_row.astype(F32)
        depth_full = jnp.broadcast_to(depth_column, (NSEC, NSEC))
        lower = jnp.sum(jnp.where(section_row == bracket, depth_full, 0.0), axis=0, keepdims=True)
        upper = jnp.sum(jnp.where(section_row == bracket + 1.0, depth_full, 0.0), axis=0, keepdims=True)
        lifted = bracket + (target[0:1] - lower) / (upper - lower)
        lift_s[...] = jnp.broadcast_to(lifted, (8, NSEC))
        to_ring(lz_copy, pltpu.make_async_copy(lift_s, lift_z.at[z], came.at[2]))

    def cross_first():
        arrived(buf_a.at[:, head], came.at[4])
        x_v[:, :FIRST] = dot(unswap[...], buf_a[:, :FIRST]).astype(BF16)
        to_plane(
            pf_copy,
            pltpu.make_async_copy(
                x_v.at[rows16(b), head], buf_p.at[rows16(b), head], came.at[5]
            ),
        )

    def lift_rows():
        arrived(lift_z, came.at[2])
        eighth = iota((8, NSEC), 0)
        ring_lift = jnp.zeros((8, NSEC), F32)
        for i in range(ZS):
            ring_lift = jnp.where(eighth == i, lift_z[i], ring_lift)
        lift_t[...] = ring_lift

        @pl.loop(1, YS)
        def _(i):
            ly_copy(i, y, (y + i) % YS).start()

        pltpu.make_async_copy(lift_t, lift_y.at[y], came.at[3]).start()

    def weigh(low, high, where):
        twice = jnp.where(iota((ROWS, NSEC), 0) // 2 == iota((ROWS, NSEC), 1), 1.0, 0.0)

        @pl.loop(low, high)
        def _(g):
            lift_columns = dot_nt(twice, lift_y[g], lax.Precision.HIGHEST)
            for i in range(ZS):
                apart = jnp.abs(lift_columns[:, i : i + 1] - where[...])
                weights[g * ZS + i] = jnp.maximum(0.0, 1.0 - apart).astype(BF16)

    def weigh_all():
        arrived(lift_y, came.at[3])
        weigh(0, FIRST // TILE // ZS, places_first)
        weigh(FIRST // TILE // ZS, YS, places)

    def mix(low, high):
        left = iota((ROWS, LANES), 1) < TILE

        @pl.loop(low // LANES, high // LANES)
        def _(m):
            at = pl.ds(pl.multiple_of(m * LANES, LANES), LANES)
            block = buf_p[:, at]
            first = dot(weights[2 * m], block)
            second = dot(weights[2 * m + 1], block)
            out_v[:, :, at] = jnp.where(left, first, second).astype(BF16).reshape(NSEC, 2, LANES)


    def mix_first():
        arrived(buf_p.at[:, head], came.at[5])
        mix(0, FIRST)

    def mix_chunk(c):
        arrived(buf_p.at[:, columns(c)], b_came.at[c])
        mix(STARTS[c], STARTS[c + 1])

    todo = {
        "h": turn_first, "b": meet, "z": first_round_ring, "r": reduce, "A": spread_reduced, "t": turn_reduced, "g": lift_tile, "p": cross_first,
        "y": lift_rows, "w": weigh_all, "m": mix_first, "o": outward, "f": forward, "M": mix_chunk,
    }
    for step in PLAN.split():
        todo[step[0]](*map(int, step[1:]))

    for n, region in enumerate(
        (
            red_a.at[: PLANE - 1],
            red_r.at[: ZS - 1],
            lift_z.at[: ZS - 1],
            lift_y.at[: YS - 1],
            buf_a.at[: ROWS - 32, head],
            buf_p.at[: ROWS - 16, head],
            buf_a.at[: ROWS - 16, tail],
            buf_s.at[: ROWS - 32, tail],
        )
    ):
        arrived(region, sent.at[n])


def per_device(sections, calibration_knots, target_offset, target_step):
    dma = pltpu.SemaphoreType.DMA
    out = pl.pallas_call(
        kernel,
        out_shape=jax.ShapeDtypeStruct((NSEC, 2, COLS), BF16),
        in_specs=[pl.BlockSpec(memory_space=pltpu.HBM)]
        + [pl.BlockSpec(memory_space=pltpu.HBM)] * 3,
        out_specs=pl.BlockSpec(memory_space=pltpu.VMEM),
        scratch_shapes=[
            pltpu.VMEM((ROWS, COLS), BF16),
            pltpu.VMEM((2, ROWS, LANES), F32),
            pltpu.VMEM((PLANE, 4, 16, LANES), BF16),
            pltpu.VMEM((PLANE, 4, 16, LANES), BF16),
            pltpu.VMEM((ZS, PLANE, 1024), BF16),
            pltpu.VMEM((ZS, PLANE, 1024), BF16),
            pltpu.VMEM((ROWS, COLS), BF16),
            pltpu.VMEM((ROWS, COLS), BF16),
            pltpu.VMEM((ROWS, COLS), BF16),
            pltpu.VMEM((TILES, ROWS, ROWS), BF16),
            pltpu.VMEM((ROWS, ROWS), F32),
            pltpu.VMEM((ROWS, ROWS), F32),
            pltpu.VMEM((ROWS, ROWS), BF16),
            pltpu.VMEM((ROWS, ROWS), BF16),
            pltpu.VMEM((8, NSEC), F32),
            pltpu.VMEM((ZS, 8, NSEC), F32),
            pltpu.VMEM((8, NSEC), F32),
            pltpu.VMEM((YS, 8, NSEC), F32),
            pltpu.SMEM((KNOTS,), jnp.int32),
            pltpu.SMEM((4, TILES), jnp.int32),
            pltpu.SMEM((4, TILES), jnp.int32),
            dma((5,)), dma((8,)), dma((6,)), dma((CHUNKS,)), dma((CHUNKS,)),
        ],
        compiler_params=pltpu.CompilerParams(collective_id=0, has_side_effects=True, vmem_limit_bytes=16 * 1024 * 1024),
    )(*(pltpu.with_memory_space_constraint(a, pltpu.HBM) for a in (sections.reshape(ROWS, COLS), calibration_knots, target_offset, target_step)))
    return out


def solution(mesh):
    return jax.shard_map(
        per_device,
        mesh=mesh,
        in_specs=(P("sec", None, "tile"), P(), P(None, "tile"), P(None, "tile")),
        out_specs=P(None, "sec", "tile"),
        check_vma=False,
    )
```

```python
import functools

import jax
import jax.numpy as jnp
from jax import lax
from jax.experimental import pallas as pl
from jax.experimental.pallas import tpu as pltpu
from jax.sharding import PartitionSpec as P

F32 = jnp.float32
BF16 = jnp.bfloat16
MESH = pl.DeviceIdType.MESH

XS, YS, ZS = 4, 4, 8
PLANE = XS * YS
NSEC = XS * YS * ZS
ROWS = 256
COLS = 2048
TILE = 64
TILES = COLS // TILE
AHEAD = 4
KNOTS = 17
LANES = 128
BLOCKS = COLS // LANES
FIRST = 512
WIDTHS = (384, 256, 256, 256, 256, 128)
CHUNKS = len(WIDTHS)
STARTS = tuple(FIRST + sum(WIDTHS[:c]) for c in range(CHUNKS + 1))
EPSILON = 1e-06


def iota(shape, axis):
    return lax.broadcasted_iota(jnp.int32, shape, axis)


def onehot(equal):
    return jnp.where(equal, 1.0, 0.0).astype(BF16)


def dot(a, b):
    return jnp.dot(a, b, preferred_element_type=F32)


def dot_nt(a, b, precision=None):
    return lax.dot_general(
        a, b, (((1,), (1,)), ((), ())), preferred_element_type=F32, precision=precision
    )


def kernel(
    x_hbm, knots_hbm, offsets_hbm, steps_hbm, out_v,
    x_v, pairs, red_s, red_a, red_b, red_r, buf_a, buf_s, buf_p, buf_m, weights, woven,
    swap, unswap, split, lift_s, lift_z, lift_t, lift_y,
    knots, offsets, steps, in_sem, sent, came, a_came, b_came,
):
    here = lax.axis_index("sec")
    b = here // ZS
    z = here % ZS
    x = b // YS
    y = b % YS

    def plane_peer(i):
        return ((x + i // YS) % XS) * YS + (y + i % YS) % YS

    def ring_peer(i):
        return (z + i) % ZS

    head = pl.ds(0, FIRST)
    tail = pl.ds(FIRST, COLS - FIRST)
    load_head = pltpu.make_async_copy(x_hbm.at[:, head], x_v.at[:, head], in_sem.at[0])
    load_tail = pltpu.make_async_copy(x_hbm.at[:, tail], x_v.at[:, tail], in_sem.at[1])
    load_head.start()
    load_tail.start()
    small = [
        pltpu.make_async_copy(source, target, in_sem.at[2 + i])
        for i, (source, target) in enumerate(
            ((knots_hbm, knots), (offsets_hbm, offsets), (steps_hbm, steps))
        )
    ]
    for copy in small:
        copy.start()

    barrier = pltpu.get_barrier_semaphore()

    @pl.loop(1, PLANE)
    def _(i):
        pl.semaphore_signal(
            barrier, inc=1, device_id={"sec": plane_peer(i) * ZS + z}, device_id_type=MESH
        )

    @pl.loop(1, ZS)
    def _(i):
        pl.semaphore_signal(
            barrier, inc=1, device_id={"sec": b * ZS + ring_peer(i)}, device_id_type=MESH
        )

    def arrived(region, semaphore):
        pltpu.make_async_copy(region, region, semaphore).wait()

    def red_a_copy(i, source, target):
        return pltpu.make_async_remote_copy(
            src_ref=red_s.at[target], dst_ref=red_a.at[source],
            send_sem=sent.at[0], recv_sem=came.at[0],
            device_id={"sec": target * ZS + z}, device_id_type=MESH,
        )

    def red_b_copy(i, source, target):
        return pltpu.make_async_remote_copy(
            src_ref=red_b.at[target], dst_ref=red_r.at[source],
            send_sem=sent.at[1], recv_sem=came.at[1],
            device_id={"sec": b * ZS + target}, device_id_type=MESH,
        )

    def columns(c):
        return pl.ds(STARTS[c], WIDTHS[c])

    def rows16(i):
        return pl.ds(pl.multiple_of(i * 16, 16), 16)

    def rows32(i):
        return pl.ds(pl.multiple_of(i * 32, 32), 32)

    def a_copy(c, i, source, target):
        return pltpu.make_async_remote_copy(
            src_ref=x_hbm.at[rows16(target), columns(c)],
            dst_ref=buf_a.at[rows16(source), columns(c)],
            send_sem=sent.at[6], recv_sem=a_came.at[c],
            device_id={"sec": target * ZS + z}, device_id_type=MESH,
        )

    def a_own(c):
        return pltpu.make_async_copy(
            x_hbm.at[rows16(b), columns(c)], buf_a.at[rows16(b), columns(c)], a_came.at[c]
        )

    def b_copy(c, i, source, target):
        return pltpu.make_async_remote_copy(
            src_ref=buf_s.at[rows32(target), columns(c)],
            dst_ref=buf_p.at[rows32(source), columns(c)],
            send_sem=sent.at[7], recv_sem=b_came.at[c],
            device_id={"sec": b * ZS + target}, device_id_type=MESH,
        )

    def b_own(c):
        return pltpu.make_async_copy(
            buf_s.at[rows32(z), columns(c)], buf_p.at[rows32(z), columns(c)], b_came.at[c]
        )

    def zf_copy(i, source, target):
        return pltpu.make_async_remote_copy(
            src_ref=buf_s.at[rows32(target), head], dst_ref=buf_a.at[rows32(source), head],
            send_sem=sent.at[4], recv_sem=came.at[4],
            device_id={"sec": b * ZS + target}, device_id_type=MESH,
        )

    def pf_copy(i, source, target):
        return pltpu.make_async_remote_copy(
            src_ref=x_v.at[rows16(target), head], dst_ref=buf_p.at[rows16(source), head],
            send_sem=sent.at[5], recv_sem=came.at[5],
            device_id={"sec": target * ZS + z}, device_id_type=MESH,
        )

    def lz_copy(i, source, target):
        return pltpu.make_async_remote_copy(
            src_ref=lift_s, dst_ref=lift_z.at[source],
            send_sem=sent.at[2], recv_sem=came.at[2],
            device_id={"sec": b * ZS + target}, device_id_type=MESH,
        )

    def ly_copy(i, source, target):
        return pltpu.make_async_remote_copy(
            src_ref=lift_t, dst_ref=lift_y.at[source],
            send_sem=sent.at[3], recv_sem=came.at[3],
            device_id={"sec": (x * YS + target) * ZS + z}, device_id_type=MESH,
        )

    row = iota((ROWS, ROWS), 0)
    col = iota((ROWS, ROWS), 1)
    swap[...] = onehot(col == (row % 16) * 16 + (row // 32) * 2 + (row // 16) % 2)
    unswap[...] = onehot(col == (row % ZS) * 32 + (row // 8) % 2 * 16 + row // 16)
    split[...] = onehot(col == (row % NSEC) // ZS * 16 + (row // NSEC) * ZS + row % ZS)

    def turn_first():
        load_head.wait()
        buf_s[:, :FIRST] = dot(swap[...], x_v[:, :FIRST]).astype(BF16)

    def meet():
        pl.semaphore_wait(barrier, PLANE - 1 + ZS - 1)

    def to_ring(copy, own):
        @pl.loop(1, ZS)
        def _(i):
            copy(i, z, ring_peer(i)).start()

        own.start()

    def to_plane(copy, own):
        @pl.loop(1, PLANE)
        def _(i):
            copy(i, b, plane_peer(i)).start()

        own.start()

    def first_round_ring():
        to_ring(
            zf_copy,
            pltpu.make_async_copy(
                buf_s.at[rows32(z), head], buf_a.at[rows32(z), head], came.at[4]
            ),
        )

    def outward(c):
        to_plane(functools.partial(a_copy, c), a_own(c))

    def forward(c):
        arrived(buf_a.at[:, columns(c)], a_came.at[c])
        buf_s[:, columns(c)] = dot(swap[...], buf_a[:, columns(c)]).astype(BF16)
        to_ring(functools.partial(b_copy, c), b_own(c))

    def reduce():
        load_tail.wait()
        n = iota((LANES, 2 * LANES), 1)
        spread = onehot(iota((LANES, 2 * LANES), 0) // 2 == (n // LANES) * 32 + n % 32)
        quarter = iota((32, LANES), 1) // 32

        @pl.loop(0, BLOCKS)
        def _(m):
            block = x_v[:, pl.ds(pl.multiple_of(m * LANES, LANES), LANES)]
            doubled = dot(block, spread)
            halves = []
            for half in range(2):
                pairs[half] = doubled[:, half * LANES : (half + 1) * LANES]
                total = jnp.zeros((32, LANES), F32)
                for v in range(4):
                    both = (
                        pairs[half, pl.ds(2 * v, 32, stride=8), :]
                        + pairs[half, pl.ds(2 * v + 1, 32, stride=8), :]
                    )
                    total = jnp.where(quarter == v, both, total)
                halves.append(total * 0.25)
            for tr in range(4):
                both = jnp.concatenate([h[8 * tr : 8 * tr + 8] for h in halves], axis=0)
                red_s[tr * 4 + m // 4, m % 4] = both.astype(BF16)
    def spread_reduced():
        to_plane(red_a_copy, pltpu.make_async_copy(red_s.at[b], red_a.at[b], came.at[0]))

    def turn_reduced():
        arrived(red_a, came.at[0])
        turn = onehot(col == (row % 16) * 16 + row // 16)
        for pair in range(4):
            mixed = dot(turn, red_a[:, pair].reshape(ROWS, LANES)).astype(BF16)
            for low in range(2):
                for u in range(8):
                    at = (low * 8 + u) * 16
                    red_b[pair * 2 + low, :, u * LANES : (u + 1) * LANES] = mixed[at : at + 16]
        to_ring(red_b_copy, pltpu.make_async_copy(red_b.at[z], red_r.at[z], came.at[1]))

    def lift_tile():
        arrived(red_r, came.at[1])
        for copy in small:
            copy.wait()

        small_row = iota((NSEC, NSEC), 0)
        small_col = iota((NSEC, NSEC), 1)
        natural = onehot(small_col == (small_row % ZS) * PLANE + small_row // ZS)
        pixels = dot(natural, red_r[...].reshape(NSEC, 1024)).astype(BF16)
        gram = dot_nt(pixels, pixels)
        sums = dot_nt(jnp.ones((8, 1024), BF16), pixels)
        samples = 1024.0

        def diagonal(k):
            kept = jnp.where(small_row == small_col + k, gram, 0.0)
            return jnp.broadcast_to(jnp.sum(kept, axis=0, keepdims=True), (8, NSEC))

        lane = iota((8, NSEC), 1)

        def ahead(values, k):
            return jnp.where(lane < NSEC - k, pltpu.roll(values, NSEC - k, 1), 0.0)

        squares = diagonal(0)
        mean_first = sums / samples
        var_first = squares / samples - mean_first * mean_first
        knot_values = [jnp.full((8, NSEC), knots[j], jnp.int32).astype(F32) / 1000.0 for j in range(KNOTS)]
        numerator = jnp.zeros((8, NSEC), F32)
        denominator = jnp.zeros((8, NSEC), F32)
        for k in range(1, AHEAD + 1):
            mean_second = ahead(sums, k) / samples
            var_second = ahead(squares, k) / samples - mean_second * mean_second
            covariance = diagonal(k) / samples - mean_first * mean_second
            correlation = covariance / jnp.sqrt(var_first * var_second + EPSILON)
            distance = jnp.zeros((8, NSEC), F32)
            for j in range(KNOTS):
                knot = -1.0 + j * (2.0 / (KNOTS - 1))
                hat = jnp.maximum(0.0, 1.0 - jnp.abs(correlation - knot) * ((KNOTS - 1) / 2.0))
                distance = distance + hat * knot_values[j]
            usable = lane < NSEC - k
            numerator = numerator + jnp.where(usable, k * distance, 0.0)
            denominator = denominator + jnp.where(usable, float(k * k), 0.0)
        thickness = numerator / jnp.maximum(denominator, 1.0)

        def behind(values, k):
            return jnp.where(lane >= k, pltpu.roll(values, k, 1), 0.0)

        depths = behind(thickness, 1)
        reach = 1
        while reach < NSEC:
            depths = depths + behind(depths, reach)
            reach *= 2

        depth_rows = jnp.broadcast_to(depths[0:1], (NSEC, NSEC))
        depth_column = jnp.sum(jnp.where(small_row == small_col, depth_rows, 0.0), axis=1, keepdims=True)
        deepest = jnp.sum(jnp.where(lane == NSEC - 1, depths, 0.0), axis=1, keepdims=True)
        offset = offsets[x, y * ZS + z]
        stride = steps[x, y * ZS + z]
        fraction = (offset + lane * stride).astype(F32) / (64.0 * NSEC)
        target = deepest * fraction
        target_row = jnp.broadcast_to(target[0:1], (NSEC, NSEC))
        at_or_above = (depth_column <= target_row) & (small_row >= 1)
        bracket = jnp.sum(jnp.where(at_or_above, 1.0, 0.0), axis=0, keepdims=True)
        bracket = jnp.minimum(bracket, float(NSEC - 2))
        section_row = small_row.astype(F32)
        depth_full = jnp.broadcast_to(depth_column, (NSEC, NSEC))
        lower = jnp.sum(jnp.where(section_row == bracket, depth_full, 0.0), axis=0, keepdims=True)
        upper = jnp.sum(jnp.where(section_row == bracket + 1.0, depth_full, 0.0), axis=0, keepdims=True)
        lifted = bracket + (target[0:1] - lower) / (upper - lower)
        lift_s[...] = jnp.broadcast_to(lifted, (8, NSEC))
        to_ring(lz_copy, pltpu.make_async_copy(lift_s, lift_z.at[z], came.at[2]))

    def cross_first():
        arrived(buf_a.at[:, head], came.at[4])
        x_v[:, :FIRST] = dot(unswap[...], buf_a[:, :FIRST]).astype(BF16)
        to_plane(
            pf_copy,
            pltpu.make_async_copy(
                x_v.at[rows16(b), head], buf_p.at[rows16(b), head], came.at[5]
            ),
        )

    def lift_rows():
        arrived(lift_z, came.at[2])
        eighth = iota((8, NSEC), 0)
        ring_lift = jnp.zeros((8, NSEC), F32)
        for i in range(ZS):
            ring_lift = jnp.where(eighth == i, lift_z[i], ring_lift)
        lift_t[...] = ring_lift

        @pl.loop(1, YS)
        def _(i):
            ly_copy(i, y, (y + i) % YS).start()

        pltpu.make_async_copy(lift_t, lift_y.at[y], came.at[3]).start()

    def weigh(low, high, places):
        same = jnp.where(iota((NSEC, NSEC), 0) == iota((NSEC, NSEC), 1), 1.0, 0.0)

        @pl.loop(low, high)
        def _(g):
            lift_columns = dot_nt(same, lift_y[g], lax.Precision.HIGHEST)
            for i in range(ZS):
                apart = jnp.abs(lift_columns[:, i : i + 1] - places)
                weights[g * ZS + i] = jnp.maximum(0.0, 1.0 - apart).astype(BF16)

    def weigh_all():
        arrived(lift_y, came.at[3])
        at = iota((NSEC, NSEC), 1)
        weigh(0, FIRST // TILE // ZS, at.astype(F32))
        weigh(FIRST // TILE // ZS, YS, ((at % PLANE) * ZS + at // PLANE).astype(F32))

    def mix(low, high, halves):
        left = iota((NSEC, 2 * LANES), 1) % LANES < TILE

        @pl.loop(low // LANES, high // LANES)
        def _(m):
            at = pl.ds(pl.multiple_of(m * LANES, LANES), LANES)
            block = jnp.concatenate(halves(at), axis=1)
            both = dot(weights[pl.ds(2 * m, 2)].reshape(2 * NSEC, NSEC), block)
            mixed = jnp.where(left, both[:NSEC], both[NSEC:])
            slot = m % 2
            woven[slot, pl.ds(0, NSEC, stride=2), :] = mixed[:, :LANES]
            woven[slot, pl.ds(1, NSEC, stride=2), :] = mixed[:, LANES:]
            out_v[:, :, at] = woven[slot].astype(BF16).reshape(NSEC, 2, LANES)

    def split_first():
        arrived(buf_p.at[:, head], came.at[5])
        buf_m[...] = dot(split[...], buf_p[:, head]).astype(BF16)

    def mix_first():
        mix(0, FIRST, lambda at: (buf_m[:NSEC, at], buf_m[NSEC:, at]))

    def mix_chunk(c):
        def halves(at):
            parts = buf_p[:, at].reshape(ZS, 2, PLANE, LANES)
            return parts[:, 0].reshape(NSEC, LANES), parts[:, 1].reshape(NSEC, LANES)

        arrived(buf_p.at[:, columns(c)], b_came.at[c])
        mix(STARTS[c], STARTS[c + 1], halves)

    turn_first()
    reduce()
    meet()
    first_round_ring()
    spread_reduced()
    outward(0)
    outward(1)
    turn_reduced()
    forward(0)
    outward(2)
    cross_first()
    outward(3)
    lift_tile()
    forward(1)
    outward(4)
    forward(2)
    outward(5)
    forward(3)
    lift_rows()
    forward(4)
    forward(5)
    split_first()
    weigh_all()
    mix_first()
    mix_chunk(0)
    mix_chunk(1)
    mix_chunk(2)
    mix_chunk(3)
    mix_chunk(4)
    mix_chunk(5)

    for n, region in enumerate(
        (
            red_a.at[: PLANE - 1],
            red_r.at[: ZS - 1],
            lift_z.at[: ZS - 1],
            lift_y.at[: YS - 1],
            buf_a.at[: ROWS - 32, head],
            buf_p.at[: ROWS - 16, head],
            buf_a.at[: ROWS - 16, tail],
            buf_s.at[: ROWS - 32, tail],
        )
    ):
        arrived(region, sent.at[n])


def per_device(sections, calibration_knots, target_offset, target_step):
    dma = pltpu.SemaphoreType.DMA
    out = pl.pallas_call(
        kernel,
        out_shape=jax.ShapeDtypeStruct((NSEC, 2, COLS), BF16),
        in_specs=[pl.BlockSpec(memory_space=pltpu.HBM)]
        + [pl.BlockSpec(memory_space=pltpu.HBM)] * 3,
        out_specs=pl.BlockSpec(memory_space=pltpu.VMEM),
        scratch_shapes=[
            pltpu.VMEM((ROWS, COLS), BF16),
            pltpu.VMEM((2, ROWS, LANES), F32),
            pltpu.VMEM((PLANE, 4, 16, LANES), BF16),
            pltpu.VMEM((PLANE, 4, 16, LANES), BF16),
            pltpu.VMEM((ZS, PLANE, 1024), BF16),
            pltpu.VMEM((ZS, PLANE, 1024), BF16),
            pltpu.VMEM((ROWS, COLS), BF16),
            pltpu.VMEM((ROWS, COLS), BF16),
            pltpu.VMEM((ROWS, COLS), BF16),
            pltpu.VMEM((ROWS, FIRST), BF16),
            pltpu.VMEM((TILES, NSEC, NSEC), BF16),
            pltpu.VMEM((2, ROWS, LANES), F32),
            pltpu.VMEM((ROWS, ROWS), BF16),
            pltpu.VMEM((ROWS, ROWS), BF16),
            pltpu.VMEM((ROWS, ROWS), BF16),
            pltpu.VMEM((8, NSEC), F32),
            pltpu.VMEM((ZS, 8, NSEC), F32),
            pltpu.VMEM((8, NSEC), F32),
            pltpu.VMEM((YS, 8, NSEC), F32),
            pltpu.SMEM((KNOTS,), jnp.int32),
            pltpu.SMEM((4, TILES), jnp.int32),
            pltpu.SMEM((4, TILES), jnp.int32),
            dma((5,)), dma((8,)), dma((6,)), dma((CHUNKS,)), dma((CHUNKS,)),
        ],
        compiler_params=pltpu.CompilerParams(collective_id=0, has_side_effects=True, vmem_limit_bytes=16 * 1024 * 1024),
    )(*(pltpu.with_memory_space_constraint(a, pltpu.HBM) for a in (sections.reshape(ROWS, COLS), calibration_knots, target_offset, target_step)))
    return out


def solution(mesh):
    return jax.shard_map(
        per_device,
        mesh=mesh,
        in_specs=(P("sec", None, "tile"), P(), P(None, "tile"), P(None, "tile")),
        out_specs=P(None, "sec", "tile"),
        check_vma=False,
    )
```

```python
import functools

import jax
import jax.numpy as jnp
from jax import lax
from jax.experimental import pallas as pl
from jax.experimental.pallas import tpu as pltpu
from jax.sharding import PartitionSpec as P

F32 = jnp.float32
BF16 = jnp.bfloat16
MESH = pl.DeviceIdType.MESH

XS, YS, ZS = 4, 4, 8
PLANE = XS * YS
NSEC = XS * YS * ZS
ROWS = 256
COLS = 2048
TILE = 64
TILES = COLS // TILE
AHEAD = 4
KNOTS = 17
LANES = 128
BLOCKS = COLS // LANES
FIRST = 768
WIDTHS = (256, 256, 256, 256, 256)
CHUNKS = len(WIDTHS)
STARTS = tuple(FIRST + sum(WIDTHS[:c]) for c in range(CHUNKS + 1))
EPSILON = 1e-06


def iota(shape, axis):
    return lax.broadcasted_iota(jnp.int32, shape, axis)


def onehot(equal):
    return jnp.where(equal, 1.0, 0.0).astype(BF16)


def dot(a, b):
    return jnp.dot(a, b, preferred_element_type=F32)


def dot_nt(a, b, precision=None):
    return lax.dot_general(
        a, b, (((1,), (1,)), ((), ())), preferred_element_type=F32, precision=precision
    )


def kernel(
    x_hbm, knots_hbm, offsets_hbm, steps_hbm, out_v,
    x_v, pairs, red_s, red_a, red_b, red_r, buf_a, buf_s, buf_p, buf_m, weights, woven,
    swap, unswap, split, lift_s, lift_z, lift_t, lift_y,
    knots, offsets, steps, in_sem, sent, came, a_came, b_came,
):
    here = lax.axis_index("sec")
    b = here // ZS
    z = here % ZS
    x = b // YS
    y = b % YS

    def plane_peer(i):
        return ((x + i // YS) % XS) * YS + (y + i % YS) % YS

    def ring_peer(i):
        return (z + i) % ZS

    head = pl.ds(0, FIRST)
    tail = pl.ds(FIRST, COLS - FIRST)
    load_head = pltpu.make_async_copy(x_hbm.at[:, head], x_v.at[:, head], in_sem.at[0])
    load_tail = pltpu.make_async_copy(x_hbm.at[:, tail], x_v.at[:, tail], in_sem.at[1])
    load_head.start()
    load_tail.start()
    small = [
        pltpu.make_async_copy(source, target, in_sem.at[2 + i])
        for i, (source, target) in enumerate(
            ((knots_hbm, knots), (offsets_hbm, offsets), (steps_hbm, steps))
        )
    ]
    for copy in small:
        copy.start()

    barrier = pltpu.get_barrier_semaphore()

    @pl.loop(1, PLANE)
    def _(i):
        pl.semaphore_signal(
            barrier, inc=1, device_id={"sec": plane_peer(i) * ZS + z}, device_id_type=MESH
        )

    @pl.loop(1, ZS)
    def _(i):
        pl.semaphore_signal(
            barrier, inc=1, device_id={"sec": b * ZS + ring_peer(i)}, device_id_type=MESH
        )

    def arrived(region, semaphore):
        pltpu.make_async_copy(region, region, semaphore).wait()

    def red_a_copy(i, source, target):
        return pltpu.make_async_remote_copy(
            src_ref=red_s.at[target], dst_ref=red_a.at[source],
            send_sem=sent.at[0], recv_sem=came.at[0],
            device_id={"sec": target * ZS + z}, device_id_type=MESH,
        )

    def red_b_copy(i, source, target):
        return pltpu.make_async_remote_copy(
            src_ref=red_b.at[target], dst_ref=red_r.at[source],
            send_sem=sent.at[1], recv_sem=came.at[1],
            device_id={"sec": b * ZS + target}, device_id_type=MESH,
        )

    def columns(c):
        return pl.ds(STARTS[c], WIDTHS[c])

    def rows16(i):
        return pl.ds(pl.multiple_of(i * 16, 16), 16)

    def rows32(i):
        return pl.ds(pl.multiple_of(i * 32, 32), 32)

    def a_copy(c, i, source, target):
        return pltpu.make_async_remote_copy(
            src_ref=x_hbm.at[rows16(target), columns(c)],
            dst_ref=buf_a.at[rows16(source), columns(c)],
            send_sem=sent.at[6], recv_sem=a_came.at[c],
            device_id={"sec": target * ZS + z}, device_id_type=MESH,
        )

    def a_own(c):
        return pltpu.make_async_copy(
            x_hbm.at[rows16(b), columns(c)], buf_a.at[rows16(b), columns(c)], a_came.at[c]
        )

    def b_copy(c, i, source, target):
        return pltpu.make_async_remote_copy(
            src_ref=buf_s.at[rows32(target), columns(c)],
            dst_ref=buf_p.at[rows32(source), columns(c)],
            send_sem=sent.at[7], recv_sem=b_came.at[c],
            device_id={"sec": b * ZS + target}, device_id_type=MESH,
        )

    def b_own(c):
        return pltpu.make_async_copy(
            buf_s.at[rows32(z), columns(c)], buf_p.at[rows32(z), columns(c)], b_came.at[c]
        )

    def zf_copy(i, source, target):
        return pltpu.make_async_remote_copy(
            src_ref=buf_s.at[rows32(target), head], dst_ref=buf_a.at[rows32(source), head],
            send_sem=sent.at[4], recv_sem=came.at[4],
            device_id={"sec": b * ZS + target}, device_id_type=MESH,
        )

    def pf_copy(i, source, target):
        return pltpu.make_async_remote_copy(
            src_ref=x_v.at[rows16(target), head], dst_ref=buf_p.at[rows16(source), head],
            send_sem=sent.at[5], recv_sem=came.at[5],
            device_id={"sec": target * ZS + z}, device_id_type=MESH,
        )

    def lz_copy(i, source, target):
        return pltpu.make_async_remote_copy(
            src_ref=lift_s, dst_ref=lift_z.at[source],
            send_sem=sent.at[2], recv_sem=came.at[2],
            device_id={"sec": b * ZS + target}, device_id_type=MESH,
        )

    def ly_copy(i, source, target):
        return pltpu.make_async_remote_copy(
            src_ref=lift_t, dst_ref=lift_y.at[source],
            send_sem=sent.at[3], recv_sem=came.at[3],
            device_id={"sec": (x * YS + target) * ZS + z}, device_id_type=MESH,
        )

    row = iota((ROWS, ROWS), 0)
    col = iota((ROWS, ROWS), 1)
    swap[...] = onehot(col == (row % 16) * 16 + (row // 32) * 2 + (row // 16) % 2)
    unswap[...] = onehot(col == (row % ZS) * 32 + (row // 8) % 2 * 16 + row // 16)
    split[...] = onehot(col == (row % NSEC) // ZS * 16 + (row // NSEC) * ZS + row % ZS)

    def turn_first():
        load_head.wait()
        buf_s[:, :FIRST] = dot(swap[...], x_v[:, :FIRST]).astype(BF16)

    def meet():
        pl.semaphore_wait(barrier, PLANE - 1 + ZS - 1)

    def to_ring(copy, own):
        @pl.loop(1, ZS)
        def _(i):
            copy(i, z, ring_peer(i)).start()

        own.start()

    def to_plane(copy, own):
        @pl.loop(1, PLANE)
        def _(i):
            copy(i, b, plane_peer(i)).start()

        own.start()

    def first_round_ring():
        to_ring(
            zf_copy,
            pltpu.make_async_copy(
                buf_s.at[rows32(z), head], buf_a.at[rows32(z), head], came.at[4]
            ),
        )

    def outward(c):
        to_plane(functools.partial(a_copy, c), a_own(c))

    def forward(c):
        arrived(buf_a.at[:, columns(c)], a_came.at[c])
        buf_s[:, columns(c)] = dot(swap[...], buf_a[:, columns(c)]).astype(BF16)
        to_ring(functools.partial(b_copy, c), b_own(c))

    def reduce():
        load_tail.wait()
        n = iota((LANES, 2 * LANES), 1)
        spread = onehot(iota((LANES, 2 * LANES), 0) // 2 == (n // LANES) * 32 + n % 32)
        quarter = iota((32, LANES), 1) // 32

        @pl.loop(0, BLOCKS)
        def _(m):
            block = x_v[:, pl.ds(pl.multiple_of(m * LANES, LANES), LANES)]
            doubled = dot(block, spread)
            halves = []
            for half in range(2):
                pairs[half] = doubled[:, half * LANES : (half + 1) * LANES]
                total = jnp.zeros((32, LANES), F32)
                for v in range(4):
                    both = (
                        pairs[half, pl.ds(2 * v, 32, stride=8), :]
                        + pairs[half, pl.ds(2 * v + 1, 32, stride=8), :]
                    )
                    total = jnp.where(quarter == v, both, total)
                halves.append(total * 0.25)
            for tr in range(4):
                both = jnp.concatenate([h[8 * tr : 8 * tr + 8] for h in halves], axis=0)
                red_s[tr * 4 + m // 4, m % 4] = both.astype(BF16)
    def spread_reduced():
        to_plane(red_a_copy, pltpu.make_async_copy(red_s.at[b], red_a.at[b], came.at[0]))

    def turn_reduced():
        arrived(red_a, came.at[0])
        turn = onehot(col == (row % 16) * 16 + row // 16)
        for pair in range(4):
            mixed = dot(turn, red_a[:, pair].reshape(ROWS, LANES)).astype(BF16)
            for low in range(2):
                for u in range(8):
                    at = (low * 8 + u) * 16
                    red_b[pair * 2 + low, :, u * LANES : (u + 1) * LANES] = mixed[at : at + 16]
        to_ring(red_b_copy, pltpu.make_async_copy(red_b.at[z], red_r.at[z], came.at[1]))

    def lift_tile():
        arrived(red_r, came.at[1])
        for copy in small:
            copy.wait()

        small_row = iota((NSEC, NSEC), 0)
        small_col = iota((NSEC, NSEC), 1)
        natural = onehot(small_col == (small_row % ZS) * PLANE + small_row // ZS)
        pixels = dot(natural, red_r[...].reshape(NSEC, 1024)).astype(BF16)
        gram = dot_nt(pixels, pixels)
        sums = dot_nt(jnp.ones((8, 1024), BF16), pixels)
        samples = 1024.0

        def diagonal(k):
            kept = jnp.where(small_row == small_col + k, gram, 0.0)
            return jnp.broadcast_to(jnp.sum(kept, axis=0, keepdims=True), (8, NSEC))

        lane = iota((8, NSEC), 1)

        def ahead(values, k):
            return jnp.where(lane < NSEC - k, pltpu.roll(values, NSEC - k, 1), 0.0)

        squares = diagonal(0)
        mean_first = sums / samples
        var_first = squares / samples - mean_first * mean_first
        knot_values = [jnp.full((8, NSEC), knots[j], jnp.int32).astype(F32) / 1000.0 for j in range(KNOTS)]
        numerator = jnp.zeros((8, NSEC), F32)
        denominator = jnp.zeros((8, NSEC), F32)
        for k in range(1, AHEAD + 1):
            mean_second = ahead(sums, k) / samples
            var_second = ahead(squares, k) / samples - mean_second * mean_second
            covariance = diagonal(k) / samples - mean_first * mean_second
            correlation = covariance / jnp.sqrt(var_first * var_second + EPSILON)
            distance = jnp.zeros((8, NSEC), F32)
            for j in range(KNOTS):
                knot = -1.0 + j * (2.0 / (KNOTS - 1))
                hat = jnp.maximum(0.0, 1.0 - jnp.abs(correlation - knot) * ((KNOTS - 1) / 2.0))
                distance = distance + hat * knot_values[j]
            usable = lane < NSEC - k
            numerator = numerator + jnp.where(usable, k * distance, 0.0)
            denominator = denominator + jnp.where(usable, float(k * k), 0.0)
        thickness = numerator / jnp.maximum(denominator, 1.0)

        def behind(values, k):
            return jnp.where(lane >= k, pltpu.roll(values, k, 1), 0.0)

        depths = behind(thickness, 1)
        reach = 1
        while reach < NSEC:
            depths = depths + behind(depths, reach)
            reach *= 2

        depth_rows = jnp.broadcast_to(depths[0:1], (NSEC, NSEC))
        depth_column = jnp.sum(jnp.where(small_row == small_col, depth_rows, 0.0), axis=1, keepdims=True)
        deepest = jnp.sum(jnp.where(lane == NSEC - 1, depths, 0.0), axis=1, keepdims=True)
        offset = offsets[x, y * ZS + z]
        stride = steps[x, y * ZS + z]
        fraction = (offset + lane * stride).astype(F32) / (64.0 * NSEC)
        target = deepest * fraction
        target_row = jnp.broadcast_to(target[0:1], (NSEC, NSEC))
        at_or_above = (depth_column <= target_row) & (small_row >= 1)
        bracket = jnp.sum(jnp.where(at_or_above, 1.0, 0.0), axis=0, keepdims=True)
        bracket = jnp.minimum(bracket, float(NSEC - 2))
        section_row = small_row.astype(F32)
        depth_full = jnp.broadcast_to(depth_column, (NSEC, NSEC))
        lower = jnp.sum(jnp.where(section_row == bracket, depth_full, 0.0), axis=0, keepdims=True)
        upper = jnp.sum(jnp.where(section_row == bracket + 1.0, depth_full, 0.0), axis=0, keepdims=True)
        lifted = bracket + (target[0:1] - lower) / (upper - lower)
        lift_s[...] = jnp.broadcast_to(lifted, (8, NSEC))
        to_ring(lz_copy, pltpu.make_async_copy(lift_s, lift_z.at[z], came.at[2]))

    def cross_first():
        arrived(buf_a.at[:, head], came.at[4])
        x_v[:, :FIRST] = dot(unswap[...], buf_a[:, :FIRST]).astype(BF16)
        to_plane(
            pf_copy,
            pltpu.make_async_copy(
                x_v.at[rows16(b), head], buf_p.at[rows16(b), head], came.at[5]
            ),
        )

    def lift_rows():
        arrived(lift_z, came.at[2])
        eighth = iota((8, NSEC), 0)
        ring_lift = jnp.zeros((8, NSEC), F32)
        for i in range(ZS):
            ring_lift = jnp.where(eighth == i, lift_z[i], ring_lift)
        lift_t[...] = ring_lift

        @pl.loop(1, YS)
        def _(i):
            ly_copy(i, y, (y + i) % YS).start()

        pltpu.make_async_copy(lift_t, lift_y.at[y], came.at[3]).start()

    def weigh_all():
        arrived(lift_y, came.at[3])
        same = jnp.where(iota((NSEC, NSEC), 0) == iota((NSEC, NSEC), 1), 1.0, 0.0)
        at = iota((NSEC, NSEC), 1)
        crossed = at.astype(F32)
        ringed = ((at % PLANE) * ZS + at // PLANE).astype(F32)
        for g in range(YS):
            lift_columns = dot_nt(same, lift_y[g], lax.Precision.HIGHEST)
            for i in range(ZS):
                tile = g * ZS + i
                places = crossed if tile * TILE < FIRST else ringed
                apart = jnp.abs(lift_columns[:, i : i + 1] - places)
                weights[tile] = jnp.maximum(0.0, 1.0 - apart).astype(BF16)

    def mix(low, high, halves):
        left = iota((NSEC, 2 * LANES), 1) % LANES < TILE

        @pl.loop(low // LANES, high // LANES)
        def _(m):
            at = pl.ds(pl.multiple_of(m * LANES, LANES), LANES)
            block = jnp.concatenate(halves(at), axis=1)
            both = dot(weights[pl.ds(2 * m, 2)].reshape(2 * NSEC, NSEC), block)
            mixed = jnp.where(left, both[:NSEC], both[NSEC:])
            slot = m % 2
            woven[slot, pl.ds(0, NSEC, stride=2), :] = mixed[:, :LANES]
            woven[slot, pl.ds(1, NSEC, stride=2), :] = mixed[:, LANES:]
            out_v[:, :, at] = woven[slot].astype(BF16).reshape(NSEC, 2, LANES)

    def split_first():
        arrived(buf_p.at[:, head], came.at[5])
        buf_m[...] = dot(split[...], buf_p[:, head]).astype(BF16)

    def mix_first():
        mix(0, FIRST, lambda at: (buf_m[:NSEC, at], buf_m[NSEC:, at]))

    def mix_chunk(c):
        def halves(at):
            parts = buf_p[:, at].reshape(ZS, 2, PLANE, LANES)
            return parts[:, 0].reshape(NSEC, LANES), parts[:, 1].reshape(NSEC, LANES)

        arrived(buf_p.at[:, columns(c)], b_came.at[c])
        mix(STARTS[c], STARTS[c + 1], halves)

    turn_first()
    reduce()
    meet()
    first_round_ring()
    spread_reduced()
    outward(0)
    outward(1)
    turn_reduced()
    forward(0)
    outward(2)
    cross_first()
    outward(3)
    outward(4)
    lift_tile()
    forward(1)
    forward(2)
    forward(3)
    forward(4)
    lift_rows()
    split_first()
    weigh_all()
    mix_first()
    mix_chunk(0)
    mix_chunk(1)
    mix_chunk(2)
    mix_chunk(3)
    mix_chunk(4)

    for n, region in enumerate(
        (
            red_a.at[: PLANE - 1],
            red_r.at[: ZS - 1],
            lift_z.at[: ZS - 1],
            lift_y.at[: YS - 1],
            buf_a.at[: ROWS - 32, head],
            buf_p.at[: ROWS - 16, head],
            buf_a.at[: ROWS - 16, tail],
            buf_s.at[: ROWS - 32, tail],
        )
    ):
        arrived(region, sent.at[n])


def per_device(sections, calibration_knots, target_offset, target_step):
    dma = pltpu.SemaphoreType.DMA
    out = pl.pallas_call(
        kernel,
        out_shape=jax.ShapeDtypeStruct((NSEC, 2, COLS), BF16),
        in_specs=[pl.BlockSpec(memory_space=pltpu.HBM)]
        + [pl.BlockSpec(memory_space=pltpu.HBM)] * 3,
        out_specs=pl.BlockSpec(memory_space=pltpu.VMEM),
        scratch_shapes=[
            pltpu.VMEM((ROWS, COLS), BF16),
            pltpu.VMEM((2, ROWS, LANES), F32),
            pltpu.VMEM((PLANE, 4, 16, LANES), BF16),
            pltpu.VMEM((PLANE, 4, 16, LANES), BF16),
            pltpu.VMEM((ZS, PLANE, 1024), BF16),
            pltpu.VMEM((ZS, PLANE, 1024), BF16),
            pltpu.VMEM((ROWS, COLS), BF16),
            pltpu.VMEM((ROWS, COLS), BF16),
            pltpu.VMEM((ROWS, COLS), BF16),
            pltpu.VMEM((ROWS, FIRST), BF16),
            pltpu.VMEM((TILES, NSEC, NSEC), BF16),
            pltpu.VMEM((2, ROWS, LANES), F32),
            pltpu.VMEM((ROWS, ROWS), BF16),
            pltpu.VMEM((ROWS, ROWS), BF16),
            pltpu.VMEM((ROWS, ROWS), BF16),
            pltpu.VMEM((8, NSEC), F32),
            pltpu.VMEM((ZS, 8, NSEC), F32),
            pltpu.VMEM((8, NSEC), F32),
            pltpu.VMEM((YS, 8, NSEC), F32),
            pltpu.SMEM((KNOTS,), jnp.int32),
            pltpu.SMEM((4, TILES), jnp.int32),
            pltpu.SMEM((4, TILES), jnp.int32),
            dma((5,)), dma((8,)), dma((6,)), dma((CHUNKS,)), dma((CHUNKS,)),
        ],
        compiler_params=pltpu.CompilerParams(collective_id=0, has_side_effects=True, vmem_limit_bytes=16 * 1024 * 1024),
    )(*(pltpu.with_memory_space_constraint(a, pltpu.HBM) for a in (sections.reshape(ROWS, COLS), calibration_knots, target_offset, target_step)))
    return out


def solution(mesh):
    return jax.shard_map(
        per_device,
        mesh=mesh,
        in_specs=(P("sec", None, "tile"), P(), P(None, "tile"), P(None, "tile")),
        out_specs=P(None, "sec", "tile"),
        check_vma=False,
    )
```

```python
import functools

import jax
import jax.numpy as jnp
from jax import lax
from jax.experimental import pallas as pl
from jax.experimental.pallas import tpu as pltpu
from jax.sharding import PartitionSpec as P

F32 = jnp.float32
BF16 = jnp.bfloat16
MESH = pl.DeviceIdType.MESH

XS, YS, ZS = 4, 4, 8
PLANE = XS * YS
NSEC = XS * YS * ZS
ROWS = 256
COLS = 2048
TILE = 64
TILES = COLS // TILE
AHEAD = 4
KNOTS = 17
LANES = 128
BLOCKS = COLS // LANES
FIRST = 768
WIDTHS = (256, 256, 256, 256, 256)
CHUNKS = len(WIDTHS)
STARTS = tuple(FIRST + sum(WIDTHS[:c]) for c in range(CHUNKS + 1))
EPSILON = 1e-06


def iota(shape, axis):
    return lax.broadcasted_iota(jnp.int32, shape, axis)


def onehot(equal):
    return jnp.where(equal, 1.0, 0.0).astype(BF16)


def dot(a, b):
    return jnp.dot(a, b, preferred_element_type=F32)


def dot_nt(a, b, precision=None):
    return lax.dot_general(
        a, b, (((1,), (1,)), ((), ())), preferred_element_type=F32, precision=precision
    )


def kernel(
    x_hbm, knots_hbm, offsets_hbm, steps_hbm, out_v,
    x_v, pairs, red_s, red_a, red_b, red_r, buf_a, buf_s, buf_p, buf_m, weights, woven,
    swap, unswap, split, lift_s, lift_z, lift_t, lift_y,
    knots, offsets, steps, in_sem, sent, came, a_came, b_came,
):
    here = lax.axis_index("sec")
    b = here // ZS
    z = here % ZS
    x = b // YS
    y = b % YS

    def plane_peer(i):
        return ((x + i // YS) % XS) * YS + (y + i % YS) % YS

    def ring_peer(i):
        return (z + i) % ZS

    head = pl.ds(0, FIRST)
    tail = pl.ds(FIRST, COLS - FIRST)
    load_head = pltpu.make_async_copy(x_hbm.at[:, head], x_v.at[:, head], in_sem.at[0])
    load_tail = pltpu.make_async_copy(x_hbm.at[:, tail], x_v.at[:, tail], in_sem.at[1])
    load_head.start()
    load_tail.start()
    small = [
        pltpu.make_async_copy(source, target, in_sem.at[2 + i])
        for i, (source, target) in enumerate(
            ((knots_hbm, knots), (offsets_hbm, offsets), (steps_hbm, steps))
        )
    ]
    for copy in small:
        copy.start()

    barrier = pltpu.get_barrier_semaphore()

    @pl.loop(1, PLANE)
    def _(i):
        pl.semaphore_signal(
            barrier, inc=1, device_id={"sec": plane_peer(i) * ZS + z}, device_id_type=MESH
        )

    @pl.loop(1, ZS)
    def _(i):
        pl.semaphore_signal(
            barrier, inc=1, device_id={"sec": b * ZS + ring_peer(i)}, device_id_type=MESH
        )

    def arrived(region, semaphore):
        pltpu.make_async_copy(region, region, semaphore).wait()

    def red_a_copy(i, source, target):
        return pltpu.make_async_remote_copy(
            src_ref=red_s.at[target], dst_ref=red_a.at[source],
            send_sem=sent.at[0], recv_sem=came.at[0],
            device_id={"sec": target * ZS + z}, device_id_type=MESH,
        )

    def red_b_copy(i, source, target):
        return pltpu.make_async_remote_copy(
            src_ref=red_b.at[target], dst_ref=red_r.at[source],
            send_sem=sent.at[1], recv_sem=came.at[1],
            device_id={"sec": b * ZS + target}, device_id_type=MESH,
        )

    def columns(c):
        return pl.ds(STARTS[c], WIDTHS[c])

    def rows16(i):
        return pl.ds(pl.multiple_of(i * 16, 16), 16)

    def rows32(i):
        return pl.ds(pl.multiple_of(i * 32, 32), 32)

    def a_copy(c, i, source, target):
        return pltpu.make_async_remote_copy(
            src_ref=x_hbm.at[rows16(target), columns(c)],
            dst_ref=buf_a.at[rows16(source), columns(c)],
            send_sem=sent.at[6], recv_sem=a_came.at[c],
            device_id={"sec": target * ZS + z}, device_id_type=MESH,
        )

    def a_own(c):
        return pltpu.make_async_copy(
            x_hbm.at[rows16(b), columns(c)], buf_a.at[rows16(b), columns(c)], a_came.at[c]
        )

    def b_copy(c, i, source, target):
        return pltpu.make_async_remote_copy(
            src_ref=buf_s.at[rows32(target), columns(c)],
            dst_ref=buf_p.at[rows32(source), columns(c)],
            send_sem=sent.at[7], recv_sem=b_came.at[c],
            device_id={"sec": b * ZS + target}, device_id_type=MESH,
        )

    def b_own(c):
        return pltpu.make_async_copy(
            buf_s.at[rows32(z), columns(c)], buf_p.at[rows32(z), columns(c)], b_came.at[c]
        )

    def zf_copy(i, source, target):
        return pltpu.make_async_remote_copy(
            src_ref=buf_s.at[rows32(target), head], dst_ref=buf_a.at[rows32(source), head],
            send_sem=sent.at[4], recv_sem=came.at[4],
            device_id={"sec": b * ZS + target}, device_id_type=MESH,
        )

    def pf_copy(i, source, target):
        return pltpu.make_async_remote_copy(
            src_ref=x_v.at[rows16(target), head], dst_ref=buf_p.at[rows16(source), head],
            send_sem=sent.at[5], recv_sem=came.at[5],
            device_id={"sec": target * ZS + z}, device_id_type=MESH,
        )

    def lz_copy(i, source, target):
        return pltpu.make_async_remote_copy(
            src_ref=lift_s, dst_ref=lift_z.at[source],
            send_sem=sent.at[2], recv_sem=came.at[2],
            device_id={"sec": b * ZS + target}, device_id_type=MESH,
        )

    def ly_copy(i, source, target):
        return pltpu.make_async_remote_copy(
            src_ref=lift_t, dst_ref=lift_y.at[source],
            send_sem=sent.at[3], recv_sem=came.at[3],
            device_id={"sec": (x * YS + target) * ZS + z}, device_id_type=MESH,
        )

    row = iota((ROWS, ROWS), 0)
    col = iota((ROWS, ROWS), 1)
    swap[...] = onehot(col == (row % 16) * 16 + (row // 32) * 2 + (row // 16) % 2)


    def turn_first():
        load_head.wait()
        buf_s[:, :FIRST] = dot(swap[...], x_v[:, :FIRST]).astype(BF16)

    def meet():
        pl.semaphore_wait(barrier, PLANE - 1 + ZS - 1)

    def to_ring(copy, own):
        @pl.loop(1, ZS)
        def _(i):
            copy(i, z, ring_peer(i)).start()

        own.start()

    def to_plane(copy, own):
        @pl.loop(1, PLANE)
        def _(i):
            copy(i, b, plane_peer(i)).start()

        own.start()

    def first_round_ring():
        to_ring(
            zf_copy,
            pltpu.make_async_copy(
                buf_s.at[rows32(z), head], buf_a.at[rows32(z), head], came.at[4]
            ),
        )

    def outward(c):
        to_plane(functools.partial(a_copy, c), a_own(c))

    def forward(c):
        arrived(buf_a.at[:, columns(c)], a_came.at[c])
        buf_s[:, columns(c)] = dot(swap[...], buf_a[:, columns(c)]).astype(BF16)
        to_ring(functools.partial(b_copy, c), b_own(c))

    def reduce():
        load_tail.wait()
        n = iota((LANES, 2 * LANES), 1)
        spread = onehot(iota((LANES, 2 * LANES), 0) // 2 == (n // LANES) * 32 + n % 32)
        quarter = iota((32, LANES), 1) // 32

        @pl.loop(0, BLOCKS)
        def _(m):
            block = x_v[:, pl.ds(pl.multiple_of(m * LANES, LANES), LANES)]
            doubled = dot(block, spread)
            halves = []
            for half in range(2):
                pairs[half] = doubled[:, half * LANES : (half + 1) * LANES]
                total = jnp.zeros((32, LANES), F32)
                for v in range(4):
                    both = (
                        pairs[half, pl.ds(2 * v, 32, stride=8), :]
                        + pairs[half, pl.ds(2 * v + 1, 32, stride=8), :]
                    )
                    total = jnp.where(quarter == v, both, total)
                halves.append(total * 0.25)
            for tr in range(4):
                both = jnp.concatenate([h[8 * tr : 8 * tr + 8] for h in halves], axis=0)
                red_s[tr * 4 + m // 4, m % 4] = both.astype(BF16)
    def spread_reduced():
        to_plane(red_a_copy, pltpu.make_async_copy(red_s.at[b], red_a.at[b], came.at[0]))

    def turn_reduced():
        turn = onehot(col == (row % 16) * 16 + row // 16)
        arrived(red_a, came.at[0])
        for pair in range(4):
            mixed = dot(turn, red_a[:, pair].reshape(ROWS, LANES)).astype(BF16)
            for low in range(2):
                for u in range(8):
                    at = (low * 8 + u) * 16
                    red_b[pair * 2 + low, :, u * LANES : (u + 1) * LANES] = mixed[at : at + 16]
        to_ring(red_b_copy, pltpu.make_async_copy(red_b.at[z], red_r.at[z], came.at[1]))

    def lift_tile():
        for copy in small:
            copy.wait()
        small_row = iota((NSEC, NSEC), 0)
        small_col = iota((NSEC, NSEC), 1)
        natural = onehot(small_col == (small_row % ZS) * PLANE + small_row // ZS)
        knot_values = [jnp.full((8, NSEC), knots[j], jnp.int32).astype(F32) / 1000.0 for j in range(KNOTS)]
        lane = iota((8, NSEC), 1)
        arrived(red_r, came.at[1])

        pixels = dot(natural, red_r[...].reshape(NSEC, 1024)).astype(BF16)
        gram = dot_nt(pixels, pixels)
        sums = dot_nt(jnp.ones((8, 1024), BF16), pixels)
        samples = 1024.0

        def diagonal(k):
            kept = jnp.where(small_row == small_col + k, gram, 0.0)
            return jnp.broadcast_to(jnp.sum(kept, axis=0, keepdims=True), (8, NSEC))


        def ahead(values, k):
            return jnp.where(lane < NSEC - k, pltpu.roll(values, NSEC - k, 1), 0.0)

        squares = diagonal(0)
        mean_first = sums / samples
        var_first = squares / samples - mean_first * mean_first
        numerator = jnp.zeros((8, NSEC), F32)
        denominator = jnp.zeros((8, NSEC), F32)
        for k in range(1, AHEAD + 1):
            mean_second = ahead(sums, k) / samples
            var_second = ahead(squares, k) / samples - mean_second * mean_second
            covariance = diagonal(k) / samples - mean_first * mean_second
            correlation = covariance / jnp.sqrt(var_first * var_second + EPSILON)
            distance = jnp.zeros((8, NSEC), F32)
            for j in range(KNOTS):
                knot = -1.0 + j * (2.0 / (KNOTS - 1))
                hat = jnp.maximum(0.0, 1.0 - jnp.abs(correlation - knot) * ((KNOTS - 1) / 2.0))
                distance = distance + hat * knot_values[j]
            usable = lane < NSEC - k
            numerator = numerator + jnp.where(usable, k * distance, 0.0)
            denominator = denominator + jnp.where(usable, float(k * k), 0.0)
        thickness = numerator / jnp.maximum(denominator, 1.0)

        def behind(values, k):
            return jnp.where(lane >= k, pltpu.roll(values, k, 1), 0.0)

        depths = behind(thickness, 1)
        reach = 1
        while reach < NSEC:
            depths = depths + behind(depths, reach)
            reach *= 2

        depth_rows = jnp.broadcast_to(depths[0:1], (NSEC, NSEC))
        depth_column = jnp.sum(jnp.where(small_row == small_col, depth_rows, 0.0), axis=1, keepdims=True)
        deepest = jnp.sum(jnp.where(lane == NSEC - 1, depths, 0.0), axis=1, keepdims=True)
        offset = offsets[x, y * ZS + z]
        stride = steps[x, y * ZS + z]
        fraction = (offset + lane * stride).astype(F32) / (64.0 * NSEC)
        target = deepest * fraction
        target_row = jnp.broadcast_to(target[0:1], (NSEC, NSEC))
        at_or_above = (depth_column <= target_row) & (small_row >= 1)
        bracket = jnp.sum(jnp.where(at_or_above, 1.0, 0.0), axis=0, keepdims=True)
        bracket = jnp.minimum(bracket, float(NSEC - 2))
        section_row = small_row.astype(F32)
        depth_full = jnp.broadcast_to(depth_column, (NSEC, NSEC))
        lower = jnp.sum(jnp.where(section_row == bracket, depth_full, 0.0), axis=0, keepdims=True)
        upper = jnp.sum(jnp.where(section_row == bracket + 1.0, depth_full, 0.0), axis=0, keepdims=True)
        lifted = bracket + (target[0:1] - lower) / (upper - lower)
        lift_s[...] = jnp.broadcast_to(lifted, (8, NSEC))
        to_ring(lz_copy, pltpu.make_async_copy(lift_s, lift_z.at[z], came.at[2]))

    def cross_first():
        arrived(buf_a.at[:, head], came.at[4])
        x_v[:, :FIRST] = dot(unswap[...], buf_a[:, :FIRST]).astype(BF16)
        to_plane(
            pf_copy,
            pltpu.make_async_copy(
                x_v.at[rows16(b), head], buf_p.at[rows16(b), head], came.at[5]
            ),
        )

    def lift_rows():
        arrived(lift_z, came.at[2])
        eighth = iota((8, NSEC), 0)
        ring_lift = jnp.zeros((8, NSEC), F32)
        for i in range(ZS):
            ring_lift = jnp.where(eighth == i, lift_z[i], ring_lift)
        lift_t[...] = ring_lift

        @pl.loop(1, YS)
        def _(i):
            ly_copy(i, y, (y + i) % YS).start()

        pltpu.make_async_copy(lift_t, lift_y.at[y], came.at[3]).start()

    def weigh_all():
        arrived(lift_y, came.at[3])
        same = jnp.where(iota((NSEC, NSEC), 0) == iota((NSEC, NSEC), 1), 1.0, 0.0)
        at = iota((NSEC, NSEC), 1)
        crossed = at.astype(F32)
        ringed = ((at % PLANE) * ZS + at // PLANE).astype(F32)
        for g in range(YS):
            lift_columns = dot_nt(same, lift_y[g], lax.Precision.HIGHEST)
            for i in range(ZS):
                tile = g * ZS + i
                places = crossed if tile * TILE < FIRST else ringed
                apart = jnp.abs(lift_columns[:, i : i + 1] - places)
                weights[tile] = jnp.maximum(0.0, 1.0 - apart).astype(BF16)

    def mix(low, high, halves):
        left = iota((NSEC, 2 * LANES), 1) % LANES < TILE

        @pl.loop(low // LANES, high // LANES)
        def _(m):
            at = pl.ds(pl.multiple_of(m * LANES, LANES), LANES)
            block = jnp.concatenate(halves(at), axis=1)
            both = dot(weights[pl.ds(2 * m, 2)].reshape(2 * NSEC, NSEC), block)
            mixed = jnp.where(left, both[:NSEC], both[NSEC:])
            slot = m % 2
            woven[slot, pl.ds(0, NSEC, stride=2), :] = mixed[:, :LANES]
            woven[slot, pl.ds(1, NSEC, stride=2), :] = mixed[:, LANES:]
            out_v[:, :, at] = woven[slot].astype(BF16).reshape(NSEC, 2, LANES)

    def split_first():
        arrived(buf_p.at[:, head], came.at[5])
        buf_m[...] = dot(split[...], buf_p[:, head]).astype(BF16)

    def mix_first():
        mix(0, FIRST, lambda at: (buf_m[:NSEC, at], buf_m[NSEC:, at]))

    def mix_chunk(c):
        def halves(at):
            parts = buf_p[:, at].reshape(ZS, 2, PLANE, LANES)
            return parts[:, 0].reshape(NSEC, LANES), parts[:, 1].reshape(NSEC, LANES)

        arrived(buf_p.at[:, columns(c)], b_came.at[c])
        mix(STARTS[c], STARTS[c + 1], halves)

    turn_first()
    reduce()
    meet()
    first_round_ring()
    spread_reduced()
    outward(0)
    outward(1)
    unswap[...] = onehot(col == (row % ZS) * 32 + (row // 8) % 2 * 16 + row // 16)
    split[...] = onehot(col == (row % NSEC) // ZS * 16 + (row // NSEC) * ZS + row % ZS)
    turn_reduced()
    forward(0)
    outward(2)
    cross_first()
    outward(3)
    outward(4)
    lift_tile()
    forward(1)
    forward(2)
    forward(3)
    forward(4)
    lift_rows()
    split_first()
    weigh_all()
    mix_first()
    mix_chunk(0)
    mix_chunk(1)
    mix_chunk(2)
    mix_chunk(3)
    mix_chunk(4)

    for n, region in enumerate(
        (
            red_a.at[: PLANE - 1],
            red_r.at[: ZS - 1],
            lift_z.at[: ZS - 1],
            lift_y.at[: YS - 1],
            buf_a.at[: ROWS - 32, head],
            buf_p.at[: ROWS - 16, head],
            buf_a.at[: ROWS - 16, tail],
            buf_s.at[: ROWS - 32, tail],
        )
    ):
        arrived(region, sent.at[n])


def per_device(sections, calibration_knots, target_offset, target_step):
    dma = pltpu.SemaphoreType.DMA
    out = pl.pallas_call(
        kernel,
        out_shape=jax.ShapeDtypeStruct((NSEC, 2, COLS), BF16),
        in_specs=[pl.BlockSpec(memory_space=pltpu.HBM)]
        + [pl.BlockSpec(memory_space=pltpu.HBM)] * 3,
        out_specs=pl.BlockSpec(memory_space=pltpu.VMEM),
        scratch_shapes=[
            pltpu.VMEM((ROWS, COLS), BF16),
            pltpu.VMEM((2, ROWS, LANES), F32),
            pltpu.VMEM((PLANE, 4, 16, LANES), BF16),
            pltpu.VMEM((PLANE, 4, 16, LANES), BF16),
            pltpu.VMEM((ZS, PLANE, 1024), BF16),
            pltpu.VMEM((ZS, PLANE, 1024), BF16),
            pltpu.VMEM((ROWS, COLS), BF16),
            pltpu.VMEM((ROWS, COLS), BF16),
            pltpu.VMEM((ROWS, COLS), BF16),
            pltpu.VMEM((ROWS, FIRST), BF16),
            pltpu.VMEM((TILES, NSEC, NSEC), BF16),
            pltpu.VMEM((2, ROWS, LANES), F32),
            pltpu.VMEM((ROWS, ROWS), BF16),
            pltpu.VMEM((ROWS, ROWS), BF16),
            pltpu.VMEM((ROWS, ROWS), BF16),
            pltpu.VMEM((8, NSEC), F32),
            pltpu.VMEM((ZS, 8, NSEC), F32),
            pltpu.VMEM((8, NSEC), F32),
            pltpu.VMEM((YS, 8, NSEC), F32),
            pltpu.SMEM((KNOTS,), jnp.int32),
            pltpu.SMEM((4, TILES), jnp.int32),
            pltpu.SMEM((4, TILES), jnp.int32),
            dma((5,)), dma((8,)), dma((6,)), dma((CHUNKS,)), dma((CHUNKS,)),
        ],
        compiler_params=pltpu.CompilerParams(collective_id=0, has_side_effects=True, vmem_limit_bytes=16 * 1024 * 1024),
    )(*(pltpu.with_memory_space_constraint(a, pltpu.HBM) for a in (sections.reshape(ROWS, COLS), calibration_knots, target_offset, target_step)))
    return out


def solution(mesh):
    return jax.shard_map(
        per_device,
        mesh=mesh,
        in_specs=(P("sec", None, "tile"), P(), P(None, "tile"), P(None, "tile")),
        out_specs=P(None, "sec", "tile"),
        check_vma=False,
    )
```
